512 devices in a mesh: role: 4 (over y), dp: 8 (over x, core), tp: 16 (over z).
Axes of the slice: x: 4, y: 4, z: 16, core: 2. Of those that a mesh axis runs over, the one named last changes fastest.
Arguments:
- ref_logits: bfloat16 [4096, 77824], P(('role', 'dp'), 'tp'), may hold values from -30 to 250
- token_ids: int32 [4096], P(('role', 'dp')), may hold values from 0 to 77823
- old_logp: bfloat16 [4096], P(('role', 'dp')), may hold values from -28 to -4
- owner_of_row: int32 [4096], P(('role', 'dp')), may hold values from 0 to 31, as said below
- lengths: int32 [64], P(('role', 'dp')), may hold values from 1 to 64
- rewards: float32 [64], replicated, may hold values from 0 to 1
- group_ids: int32 [64], replicated, may hold values from 0 to 7
- pol_logits: bfloat16 [6144, 77824], P(('role', 'dp'), 'tp'), may hold values from -30 to 250
Outputs:
- grad_logits: bfloat16 [6144, 77824], P(('role', 'dp'), 'tp')
- token_loss: float32 [6144], P(('role', 'dp'))
The draws below stay inside these ranges and needn't reach their ends.
Inputs may be any that keep to these rules, and one draw needn't show every extreme that they name: `owner_of_row`: among the rows of one owner (aligned blocks of 128 rows) at most 6 name the same owner; one owner drawn from the seed is named by exactly 6 rows in every block.
All inputs are finite; a program needn't handle non-finite values.
Results may differ from the reference program's by a relative error of at most 0.001.
Values may be sent and summed in bfloat16 or wider, within the bound.
No kernel may reach another device: no remote copies, remote signals or barrier semaphores. Data moves between devices by JAX's collectives and lax.ppermute only.
A program may use at most 64 MiB of HBM per device.

```python
import math
import jax
import jax.numpy as jnp
import numpy as np
from jax import lax

V = 77824
LMAX = 64
SEQ_DEV = 2
OWNERS = 32
R_DEV = 128
ROWS = 4096
SEQS = 64
NGROUP = 8
CAP = 6
PACKED = 6144


def draw_owner_of_row(key, part):
    slot_count = OWNERS * CAP
    fixed_owner = jax.random.randint(jax.random.fold_in(key, 1), (), 0, OWNERS)
    slot_owner = jnp.arange(slot_count) // CAP

    def one_block(block_key):
        key_extra = jax.random.fold_in(block_key, 3)
        key_rank = jax.random.fold_in(block_key, 4)
        key_shuffle = jax.random.fold_in(block_key, 5)
        extra_owner = jax.random.randint(key_extra, (), 0, OWNERS)
        slot_ranks = jax.random.permutation(key_rank, slot_count)
        favoured = (slot_owner == fixed_owner) | (slot_owner == extra_owner)
        scores = slot_ranks + jnp.where(favoured, -slot_count, 0)
        picked_order = jnp.argsort(scores, stable=True)
        chosen = slot_owner[picked_order[:R_DEV]]
        return chosen[jax.random.permutation(key_shuffle, R_DEV)]
    block_keys = jax.random.split(jax.random.fold_in(key, 2), OWNERS)
    return jax.vmap(one_block)(block_keys).reshape(ROWS).astype(jnp.int32)


def draw_lengths(key, part):
    seq_index = jnp.arange(SEQS)
    block_index = seq_index // SEQ_DEV
    top_len = jnp.maximum(LMAX * (OWNERS + 3 * block_index) // (4 * OWNERS), 1)
    low_len = jnp.maximum(top_len // 2, 1)
    drawn = jax.random.randint(jax.random.fold_in(key, 7), (SEQS,), low_len, top_len + 1)
    return jnp.where(seq_index == SEQS - 1, LMAX, drawn).astype(jnp.int32)


def draw_old_logp(key, part):
    values = -16.0 + 3.0 * jax.random.truncated_normal(jax.random.fold_in(key, 12), -4.0, 4.0, (ROWS,), jnp.float32)
    return values.astype(jnp.bfloat16)


def logit_table(key, row_total):
    base_draw = jax.random.truncated_normal(jax.random.fold_in(key, 31), -6.0, 6.0, (row_total, V), jnp.float32)
    values = 3.0 * base_draw
    return values.astype(jnp.bfloat16)


def draw_ref_logits(key, part):
    return logit_table(jax.random.fold_in(key, 41), ROWS)


def draw_pol_logits(key, part):
    return logit_table(jax.random.fold_in(key, 42), PACKED)


def with_ends(entries, rng, low, high):
    longest = entries.shape.index(max(entries.shape))
    spots = []
    for shift in (0, 1):
        where = [jax.random.randint(jax.random.fold_in(rng, axis), (), 0, length) for axis, length in enumerate(entries.shape)]
        where[longest] = (where[longest] + shift) % entries.shape[longest]
        spots.append(tuple(where))
    return entries.at[spots[0]].set(low).at[spots[1]].set(high)


def ranked_wide(rng, extent, amount, lean):
    weights = [min(1 << octave, amount + 1 - (1 << octave)) * (1 << 20) // math.isqrt((1 << octave) ** lean) + 1 for octave in range((amount + 1).bit_length()) if 1 << octave <= amount]
    spread = 1 + sum(weights) // (1 << 30)
    table = np.cumsum(np.array([max(1, weight // spread) for weight in weights]))
    pick = jax.random.randint(jax.random.fold_in(rng, 1), extent, 0, int(table[len(weights) - 1]))
    start = jnp.left_shift(1, jnp.searchsorted(jnp.asarray(table, jnp.int32), pick, side="right").astype(jnp.int32))
    rank = start - 1 + jax.random.randint(jax.random.fold_in(rng, 4), extent, 0, 1 << 30) % jnp.minimum(start, amount + 1 - start)
    return jax.random.permutation(jax.random.fold_in(rng, 2), amount)[rank].astype(jnp.int32)


def setup_inputs(seed: int = 0) -> dict:
    key_list = jax.random.split(jax.random.key(seed), 9)
    ref_logits = draw_ref_logits(jax.random.fold_in(key_list[8], 71), 0)
    token_ids = with_ends(ranked_wide(key_list[1], (ROWS,), V, 2), jax.random.fold_in(key_list[1], 3), 0, V - 1).astype(jnp.int32)
    old_logp = draw_old_logp(jax.random.fold_in(key_list[8], 71), 0)
    owner_of_row = draw_owner_of_row(jax.random.fold_in(key_list[8], 71), 0)
    lengths = draw_lengths(jax.random.fold_in(key_list[8], 71), 0)
    rewards = jnp.clip(jax.random.uniform(key_list[5], (SEQS,), jnp.float32, 0.0, 1.0), 0.0, 1.0)
    group_ids = with_ends(jax.random.randint(key_list[6], (SEQS,), 0, NGROUP), jax.random.fold_in(key_list[6], 1), 0, NGROUP - 1).astype(jnp.int32)
    pol_logits = draw_pol_logits(jax.random.fold_in(key_list[8], 71), 0)
    return {"ref_logits": ref_logits, "token_ids": token_ids, "old_logp": old_logp, "owner_of_row": owner_of_row, "lengths": lengths, "rewards": rewards, "group_ids": group_ids, "pol_logits": pol_logits}


kl_weight = 0.04
low_bound = 0.8
high_bound = 1.2
dual_bound = 3.0
ratio_clamp = 20.0


def block_terms(policy, ref_rows, tok_rows, old_rows, adv_rows, valid_rows, loss_scale):
    policy = policy.astype(jnp.float32)
    ref_rows = ref_rows.astype(jnp.float32)
    peak_p = jnp.max(policy, axis=1)
    policy_exp = jnp.exp(policy - peak_p[:, None])
    total_p = jnp.sum(policy_exp, axis=1)
    peak_q = jnp.max(ref_rows, axis=1)
    total_q = jnp.sum(jnp.exp(ref_rows - peak_q[:, None]), axis=1)
    cross_sum = jnp.sum(policy_exp * (policy - ref_rows), axis=1)
    token_hit = jnp.arange(V)[None, :] == tok_rows[:, None]
    token_logit = jnp.sum(jnp.where(token_hit, policy, 0.0), axis=1)
    log_p = peak_p + jnp.log(total_p)
    log_q = peak_q + jnp.log(total_q)
    mean_gap = cross_sum / total_p
    kl_term = mean_gap - log_p + log_q
    raw_log_ratio = token_logit - log_p - old_rows.astype(jnp.float32)
    prob_ratio = jnp.exp(jnp.clip(raw_log_ratio, -ratio_clamp, ratio_clamp))
    plain_loss = -adv_rows * prob_ratio
    clipped_loss = -adv_rows * jnp.clip(prob_ratio, low_bound, high_bound)
    upper_loss = jnp.maximum(plain_loss, clipped_loss)
    dual_loss = -dual_bound * adv_rows
    negative = adv_rows < 0.0
    policy_loss = jnp.where(negative, jnp.minimum(upper_loss, dual_loss), upper_loss)
    token_losses = jnp.where(valid_rows, policy_loss + kl_weight * kl_term, 0.0)
    inside = (prob_ratio > low_bound) & (prob_ratio < high_bound)
    token_coef = jnp.where((plain_loss >= clipped_loss) | inside, plain_loss, 0.0)
    token_coef = jnp.where(negative & (upper_loss > dual_loss), 0.0, token_coef)
    token_coef = jnp.where(jnp.abs(raw_log_ratio) < ratio_clamp, token_coef, 0.0)
    policy_prob = policy_exp / total_p[:, None]
    grad_rows = token_coef[:, None] * (token_hit.astype(jnp.float32) - policy_prob)
    grad_rows = grad_rows + kl_weight * policy_prob * ((policy - ref_rows) - mean_gap[:, None])
    grad_rows = jnp.where(valid_rows[:, None], loss_scale * grad_rows, 0.0).astype(jnp.bfloat16)
    return grad_rows, token_losses


def reference(ref_logits, token_ids, old_logp, owner_of_row, lengths, rewards, group_ids, pol_logits):
    member = (group_ids[:, None] == jnp.arange(NGROUP)[None, :]).astype(jnp.float32)
    group_total = jnp.sum(member * rewards[:, None], axis=0)
    group_count = jnp.sum(member, axis=0)
    group_mean = group_total / jnp.maximum(group_count, 1.0)
    advantage = rewards - jnp.sum(member * group_mean[None, :], axis=1)
    row_index = jnp.arange(ROWS)
    sequence = row_index // LMAX
    valid = (row_index % LMAX) < lengths[sequence]
    valid_total = jnp.sum(valid.astype(jnp.float32))
    loss_scale = ROWS / valid_total
    owner_block = owner_of_row.reshape(OWNERS, R_DEV)
    owner_hot = (owner_block[:, :, None] == jnp.arange(OWNERS)[None, None, :]).astype(jnp.int32)
    earlier = jnp.cumsum(owner_hot, axis=1) - owner_hot
    row_rank = jnp.sum(earlier * owner_hot, axis=2).reshape(ROWS)
    slot = (owner_of_row * (OWNERS * CAP) + (row_index // R_DEV) * CAP + row_rank).astype(jnp.int32)
    row_adv = advantage[sequence]

    def one_block(block_args):
        block_slot, ref_rows, tok_rows, old_rows, adv_rows, valid_rows = block_args
        policy = pol_logits[block_slot]
        return block_terms(policy, ref_rows, tok_rows, old_rows, adv_rows, valid_rows, loss_scale)

    grad_blocks, loss_blocks = lax.map(one_block, (slot.reshape(OWNERS, R_DEV), ref_logits.reshape(OWNERS, R_DEV, V), token_ids.reshape(OWNERS, R_DEV), old_logp.reshape(OWNERS, R_DEV), row_adv.reshape(OWNERS, R_DEV), valid.reshape(OWNERS, R_DEV)))
    grad_logits = jnp.zeros((PACKED, V), jnp.bfloat16).at[slot].set(grad_blocks.reshape(ROWS, V))
    token_loss = jnp.zeros((PACKED,), jnp.float32).at[slot].set(loss_blocks.reshape(ROWS))
    return grad_logits, token_loss
```

```python
import functools

import jax
import jax.numpy as jnp
from jax import lax
from jax.experimental import pallas as pl
from jax.experimental.pallas import tpu as pltpu
from jax.sharding import PartitionSpec as P

kl_weight = 0.04
low_bound = 0.8
high_bound = 1.2
dual_bound = 3.0
ratio_clamp = 20.0

LANES = 128
GROUP = 4
OCTET = 8
VMEM_LIMIT = 16 * 1024 * 1024

f32 = jnp.float32
bf16 = jnp.bfloat16
i32 = jnp.int32


def iota(shape, dim):
    return lax.broadcasted_iota(i32, shape, dim)


def send_kernel(cap, ids_ref, old_ref, owner_ref, len_ref, ref_ref, send_ref):
    rows = ref_ref.shape[0]
    blocks = ref_ref.shape[1] // LANES
    owners = send_ref.shape[0]
    groups = send_ref.shape[1] // (GROUP * cap)
    seq_local = len_ref.shape[0]
    span = rows // seq_local
    me = lax.axis_index("role") * lax.axis_size("dp") + lax.axis_index("dp")

    owner = owner_ref[...].reshape(1, rows)
    hot = (iota((owners, rows), 0) == owner).astype(f32)
    before = (iota((rows, rows), 0) < iota((rows, rows), 1)).astype(bf16)
    earlier = jnp.dot(hot.astype(bf16), before, preferred_element_type=f32)
    rank = jnp.sum(earlier * hot, axis=0, keepdims=True).astype(i32)
    slot = owner * cap + rank

    lane = iota((1, rows), 1)
    tag = jnp.zeros((1, rows), i32)
    count = jnp.int32(0)
    for s in range(seq_local):
        length = len_ref[s]
        inside = (lane >= s * span) & (lane < s * span + jnp.minimum(length, span))
        tag = jnp.where(inside, me * seq_local + s + 1, tag)
        count = count + jnp.clip(length, 0, span)
    ids = ids_ref[...].reshape(1, rows)
    feature = iota((LANES, rows), 0)
    table = jnp.zeros((LANES, rows), f32)
    values = (
        (ids & 255).astype(f32),
        ((ids >> 8) & 255).astype(f32),
        (ids >> 16).astype(f32),
        old_ref[...].reshape(1, rows).astype(f32),
        tag.astype(f32),
    )
    for n, value in enumerate(values):
        table = jnp.where(feature == n, value, table)
    table = table.T.astype(bf16)
    nothing = jnp.zeros((rows, LANES), bf16)

    def block(c):
        if c < blocks:
            return ref_ref[:, c * LANES : (c + 1) * LANES]
        return table if c == blocks else nothing

    tall = GROUP * cap
    row = iota((OCTET, tall, rows), 1)
    place = iota((OCTET, tall, rows), 0) * cap + row
    pickers = []
    for o in range(owners // OCTET):
        parts = []
        for c in range(GROUP):
            mine = (row >= c * cap) & (row < (c + 1) * cap)
            hit = mine & (place + o * OCTET * cap == slot.reshape(1, 1, rows) + c * cap)
            parts.append(hit.astype(f32).reshape(OCTET * tall, rows).astype(bf16))
        pickers.append(jnp.concatenate(parts, axis=1))
    last_row = iota((OCTET, tall, LANES), 1)
    for g in range(0, groups, 2):
        right = jnp.concatenate(
            [
                jnp.concatenate([block((g + h) * GROUP + c) for h in range(2)], axis=1)
                for c in range(GROUP)
            ],
            axis=0,
        )
        for o in range(owners // OCTET):
            out = jnp.dot(pickers[o], right, preferred_element_type=f32)
            for h in range(2):
                part = out[:, h * LANES : (h + 1) * LANES].reshape(OCTET, tall, LANES)
                if (g + h + 1) * GROUP > blocks + 1:
                    first = (blocks + 1 - (g + h) * GROUP) * cap
                    part = jnp.where(last_row >= first, count.astype(f32), part)
                send_ref[
                    o * OCTET : (o + 1) * OCTET, (g + h) * tall : (g + h + 1) * tall, :
                ] = part.astype(bf16)


def policy_kernel(pol_ref, exp_ref, stat_ref):
    slots, columns = pol_ref.shape
    step = 48
    lane = iota((step, LANES), 1)

    def body(i, carry):
        at = pl.ds(pl.multiple_of(i * step, 16), step)
        top = pol_ref[at, 0:LANES].astype(f32)
        for c in range(1, columns // LANES):
            top = jnp.maximum(top, pol_ref[at, c * LANES : (c + 1) * LANES].astype(f32))
        top = jnp.max(top, axis=1, keepdims=True)
        total = jnp.zeros((step, LANES), f32)
        for c in range(columns // LANES):
            part = jnp.exp(pol_ref[at, c * LANES : (c + 1) * LANES].astype(f32) - top)
            exp_ref[at, c * LANES : (c + 1) * LANES] = part
            total = total + part
        total = jnp.sum(total, axis=1, keepdims=True)
        stat_ref[at, :] = jnp.where(lane == 0, top, jnp.where(lane == 1, total, 0.0))
        return carry

    lax.fori_loop(0, slots // step, body, 0)


def partial_kernel(cap, got_ref, pol_ref, exp_ref, stat_ref, rows_ref, part_ref, meta_ref, column_ref):
    slots, columns = pol_ref.shape
    blocks = columns // LANES
    owners = got_ref.shape[0]
    tall = GROUP * cap
    wide = OCTET * cap
    groups = got_ref.shape[1] // tall
    base = lax.axis_index("tp") * columns

    size = OCTET * tall
    a = iota((GROUP, wide, size), 0)
    b = iota((GROUP, wide, size), 1)
    target = b + cap * a
    for d in range(1, OCTET):
        target = target + jnp.where(b >= d * cap, tall - cap, 0)
    order = (target == iota((GROUP, wide, size), 2)).astype(f32).reshape(size, size).astype(bf16)
    lane = iota((wide, LANES), 1)

    def body(o, carry):
        at = pl.ds(pl.multiple_of(o * wide, 16), wide)
        from_owner = pl.ds(o * OCTET, OCTET)

        def arrived(g):
            pair = [
                got_ref[from_owner, (g + h) * tall : (g + h + 1) * tall, :]
                .astype(f32)
                .reshape(size, LANES)
                .astype(bf16)
                for h in range(2)
            ]
            return jnp.dot(order, jnp.concatenate(pair, axis=1), preferred_element_type=f32)

        token = None
        top = jnp.full((wide, LANES), -jnp.inf, f32)
        cross = jnp.zeros((wide, LANES), f32)
        picked = jnp.zeros((wide, LANES), f32)
        info = counts = None
        for g in range(groups - 2, -1, -2):
            product = arrived(g)
            pieces = {
                (g + h) * GROUP + c: product[c * wide : (c + 1) * wide, h * LANES : (h + 1) * LANES]
                for h in range(2)
                for c in range(GROUP)
            }
            if blocks in pieces:
                info, counts = pieces[blocks], pieces[blocks + 1]
                token = (info[:, 0:1] + 256.0 * info[:, 1:2] + 65536.0 * info[:, 2:3]).astype(i32) - base
            for c in sorted(n for n in pieces if n < blocks):
                q = pieces[c]
                span = slice(c * LANES, (c + 1) * LANES)
                z = pol_ref[at, span].astype(f32)
                rows_ref[at, span] = q.astype(bf16)
                top = jnp.maximum(top, q)
                cross = cross + exp_ref[at, span] * (z - q)
                picked = picked + jnp.where(lane == token - c * LANES, z, 0.0)
        top = jnp.max(top, axis=1, keepdims=True)
        total = jnp.zeros((wide, LANES), f32)
        for c in range(blocks):
            total = total + jnp.exp(rows_ref[at, c * LANES : (c + 1) * LANES].astype(f32) - top)
        sums = (
            jnp.sum(cross, axis=1, keepdims=True),
            jnp.sum(picked, axis=1, keepdims=True),
            top,
            jnp.sum(total, axis=1, keepdims=True),
        )
        out = jnp.where(lane < 2, stat_ref[at, :], 0.0)
        for n, value in enumerate(sums):
            out = jnp.where(lane == 2 + n, value, out)
        for n, value in enumerate((info[:, 3:4], info[:, 4:5], token.astype(f32), counts[:, 0:1])):
            out = jnp.where(lane == 8 + n, value, out)
        column_ref[at, :] = out
        return carry

    lax.fori_loop(0, owners // OCTET, body, 0)
    column_ref[slots:, :] = jnp.zeros((column_ref.shape[0] - slots, LANES), f32)
    turned = column_ref[...].T
    part_ref[...] = jnp.broadcast_to(turned[None, 0:8, :], part_ref.shape)
    meta_ref[...] = turned[8:16, :]


def grad_kernel(cap, row_total, all_ref, mine_ref, meta_ref, rewards_ref, group_ref, pol_ref, rows_ref, exp_ref, grad_ref, loss_ref, turn_ref, column_ref):
    slots, columns = pol_ref.shape
    blocks = columns // LANES
    seqs = rewards_ref.shape[0]
    wide = OCTET * cap
    padded = meta_ref.shape[1]

    rewards = rewards_ref[...].reshape(1, seqs)
    groups = group_ref[...].reshape(1, seqs)
    diagonal = iota((seqs, seqs), 0) == iota((seqs, seqs), 1)
    group_down = jnp.sum(jnp.where(diagonal, groups, 0), axis=1, keepdims=True)
    reward_down = jnp.sum(jnp.where(diagonal, rewards, 0.0), axis=1, keepdims=True)
    same = (group_down == groups).astype(f32)
    mean = jnp.sum(same * rewards, axis=1, keepdims=True) / jnp.sum(same, axis=1, keepdims=True)
    advantage = reward_down - mean

    old, tag, token, counts = (meta_ref[n : n + 1, :] for n in range(4))
    valid = tag > 0.5
    adv = jnp.sum(
        jnp.where(iota((seqs, padded), 0) + 1 == tag.astype(i32), advantage, 0.0), axis=0, keepdims=True
    )
    valid_total = jnp.sum(jnp.where(iota((1, padded), 1) < slots, counts, 0.0)) / cap

    peaks, totals, crosses, tokens, peaks_q, totals_q = (all_ref[:, n, :] for n in range(6))
    peak = jnp.max(peaks, axis=0, keepdims=True)
    shift = jnp.exp(peaks - peak)
    total = jnp.sum(totals * shift, axis=0, keepdims=True)
    gap = jnp.sum(crosses * shift, axis=0, keepdims=True) / total
    peak_q = jnp.max(peaks_q, axis=0, keepdims=True)
    total_q = jnp.sum(totals_q * jnp.exp(peaks_q - peak_q), axis=0, keepdims=True)
    log_p = peak + jnp.log(total)
    log_q = peak_q + jnp.log(total_q)
    kl_term = gap - log_p + log_q
    raw = jnp.sum(tokens, axis=0, keepdims=True) - log_p - old
    ratio = jnp.exp(jnp.clip(raw, -ratio_clamp, ratio_clamp))
    plain = -adv * ratio
    clipped = -adv * jnp.clip(ratio, low_bound, high_bound)
    upper = jnp.maximum(plain, clipped)
    dual = -dual_bound * adv
    negative = adv < 0.0
    loss = jnp.where(negative, jnp.minimum(upper, dual), upper)
    loss_ref[...] = jnp.where(valid, loss + kl_weight * kl_term, 0.0)[:, :slots].reshape(slots)
    inside = (ratio > low_bound) & (ratio < high_bound)
    coef = jnp.where((plain >= clipped) | inside, plain, 0.0)
    coef = jnp.where(negative & (upper > dual), 0.0, coef)
    coef = jnp.where(jnp.abs(raw) < ratio_clamp, coef, 0.0)
    scale = jnp.where(valid, row_total / valid_total, 0.0)
    factor = scale * (jnp.exp(mine_ref[0, 0:1, :] - peak) / total)
    turn_ref[...] = jnp.zeros(turn_ref.shape, f32)
    for n, value in enumerate((factor * kl_weight, factor * coef, scale * coef, gap, token)):
        turn_ref[n : n + 1, :] = value
    column_ref[...] = turn_ref[...].T
    lane = iota((wide, LANES), 1)

    def body(o, carry):
        at = pl.ds(pl.multiple_of(o * wide, 16), wide)
        slope, level, spike, gaps, col = (
            jnp.broadcast_to(column_ref[at, n : n + 1], (wide, LANES)) for n in range(5)
        )
        where = col.astype(i32)
        for c in range(blocks):
            span = slice(c * LANES, (c + 1) * LANES)
            z = pol_ref[at, span].astype(f32)
            q = rows_ref[at, span].astype(f32)
            out = exp_ref[at, span] * (slope * ((z - q) - gaps) - level)
            out = out + jnp.where(lane == where - c * LANES, spike, 0.0)
            grad_ref[at, span] = out.astype(bf16)
        return carry

    lax.fori_loop(0, slots // wide, body, 0)


def call(kernel, out_shape, n_in, scratch=(), smem=(), cost=None):
    vmem = pl.BlockSpec(memory_space=pltpu.VMEM)
    scalar = pl.BlockSpec(memory_space=pltpu.SMEM)
    return pl.pallas_call(
        kernel,
        out_shape=out_shape,
        in_specs=[scalar if n in smem else vmem for n in range(n_in)],
        out_specs=jax.tree.map(lambda _: vmem, out_shape),
        scratch_shapes=list(scratch),
        compiler_params=pltpu.CompilerParams(vmem_limit_bytes=VMEM_LIMIT),
        cost_estimate=cost,
    )


def shards(ref_logits, token_ids, old_logp, owner_of_row, lengths, rewards, group_ids, pol_logits):
    owners = lax.axis_size("role") * lax.axis_size("dp")
    peers = lax.axis_size("tp")
    rows, columns = ref_logits.shape
    slots = pol_logits.shape[0]
    cap = slots // owners
    blocks = columns // LANES
    groups = -(-(blocks + 2) // (2 * GROUP)) * 2
    deep = groups * GROUP * cap
    padded = -(-slots // LANES) * LANES
    shape = jax.ShapeDtypeStruct
    everyone = ("role", "dp")

    send = call(
        functools.partial(send_kernel, cap), shape((owners, deep, LANES), bf16), 5, smem=(3,)
    )(token_ids, old_logp, owner_of_row, lengths, ref_logits)
    got = lax.all_to_all(send, everyone, split_axis=0, concat_axis=0, tiled=True)
    exps, stats = call(
        policy_kernel,
        (shape((slots, columns), f32), shape((slots, LANES), f32)),
        1,
        cost=pl.CostEstimate(
            flops=8 * slots * columns, bytes_accessed=6 * slots * columns, transcendentals=slots * columns
        ),
    )(pol_logits)
    got_rows, parts, meta = call(
        functools.partial(partial_kernel, cap),
        (shape((slots, columns), bf16), shape((peers, 8, padded), f32), shape((8, padded), f32)),
        4,
        scratch=(pltpu.VMEM((padded, LANES), f32),),
    )(got, pol_logits, exps, stats)
    everything = lax.all_to_all(parts, "tp", split_axis=0, concat_axis=0, tiled=True)
    return call(
        functools.partial(grad_kernel, cap, float(rows * owners)),
        (shape((slots, columns), bf16), shape((slots,), f32)),
        8,
        scratch=(pltpu.VMEM((LANES, padded), f32), pltpu.VMEM((padded, LANES), f32)),
    )(everything, parts, meta, rewards, group_ids, pol_logits, got_rows, exps)


def solution(mesh):
    return jax.shard_map(
        shards,
        mesh=mesh,
        in_specs=(
            P(("role", "dp"), "tp"),
            P(("role", "dp")),
            P(("role", "dp")),
            P(("role", "dp")),
            P(("role", "dp")),
            P(),
            P(),
            P(("role", "dp"), "tp"),
        ),
        out_specs=(P(("role", "dp"), "tp"), P(("role", "dp"))),
        check_vma=False,
    )
```

```python
import functools

import jax
import jax.numpy as jnp
from jax import lax
from jax.experimental import pallas as pl
from jax.experimental.pallas import tpu as pltpu
from jax.sharding import PartitionSpec as P

kl_weight = 0.04
low_bound = 0.8
high_bound = 1.2
dual_bound = 3.0
ratio_clamp = 20.0

LANES = 128
GROUP = 4
OCTET = 8
VMEM_LIMIT = 16 * 1024 * 1024
WHOLE_VMEM = 60 * 1024 * 1024

f32 = jnp.float32
bf16 = jnp.bfloat16
i32 = jnp.int32


def iota(shape, dim):
    return lax.broadcasted_iota(i32, shape, dim)


def send_kernel(
    cap, ids_hbm, old_hbm, owner_hbm, len_hbm, ref_hbm, send_hbm, ids_ref, old_ref, owner_ref, len_ref, ref_ref, send_ref, small, load, store
):
    rows = ref_ref.shape[0]
    blocks = ref_ref.shape[1] // LANES
    owners = send_ref.shape[0]
    tall = GROUP * cap
    groups = send_ref.shape[1] // tall
    seq_local = len_ref.shape[0]
    span = rows // seq_local
    me = lax.axis_index("role") * lax.axis_size("dp") + lax.axis_index("dp")

    smalls = [
        pltpu.make_async_copy(source, target, small.at[n])
        for n, (source, target) in enumerate(
            ((owner_hbm, owner_ref), (ids_hbm, ids_ref), (old_hbm, old_ref), (len_hbm, len_ref))
        )
    ]
    loads = []
    for n, g in enumerate(range(0, groups, 2)):
        part = slice(g * GROUP * LANES, min((g + 2) * GROUP, blocks) * LANES)
        loads.append(pltpu.make_async_copy(ref_hbm.at[:, part], ref_ref.at[:, part], load.at[n]))
    for copy in smalls + loads:
        copy.start()

    before = (iota((rows, rows), 0) < iota((rows, rows), 1)).astype(bf16)
    lane = iota((1, rows), 1)
    feature = iota((LANES, rows), 0)
    smalls[0].wait()
    owner = owner_ref[...].reshape(1, rows)
    hot = (iota((owners, rows), 0) == owner).astype(f32)
    earlier = jnp.dot(hot.astype(bf16), before, preferred_element_type=f32)
    rank = jnp.sum(earlier * hot, axis=0, keepdims=True).astype(i32)
    slot = owner * cap + rank

    for copy in smalls[1:]:
        copy.wait()
    tag = jnp.zeros((1, rows), i32)
    count = jnp.int32(0)
    for s in range(seq_local):
        length = len_ref[s]
        inside = (lane >= s * span) & (lane < s * span + jnp.minimum(length, span))
        tag = jnp.where(inside, me * seq_local + s + 1, tag)
        count = count + jnp.clip(length, 0, span)
    ids = ids_ref[...].reshape(1, rows)
    table = jnp.zeros((LANES, rows), f32)
    values = (
        (ids & 255).astype(f32),
        ((ids >> 8) & 255).astype(f32),
        (ids >> 16).astype(f32),
        old_ref[...].reshape(1, rows).astype(f32),
        tag.astype(f32),
    )
    for n, value in enumerate(values):
        table = jnp.where(feature == n, value, table)
    table = table.T.astype(bf16)
    nothing = jnp.zeros((rows, LANES), bf16)

    def block(c):
        if c < blocks:
            return ref_ref[:, c * LANES : (c + 1) * LANES]
        return table if c == blocks else nothing

    row = iota((OCTET, tall, rows), 1)
    place = iota((OCTET, tall, rows), 0) * cap + row
    pickers = []
    for o in range(owners // OCTET):
        parts = []
        for c in range(GROUP):
            mine = (row >= c * cap) & (row < (c + 1) * cap)
            hit = mine & (place + o * OCTET * cap == slot.reshape(1, 1, rows) + c * cap)
            parts.append(hit.astype(f32).reshape(OCTET * tall, rows).astype(bf16))
        pickers.append(jnp.concatenate(parts, axis=1))
    last_row = iota((OCTET, tall, LANES), 1)
    stores = []
    for n, g in enumerate(range(0, groups, 2)):
        loads[n].wait()
        right = jnp.concatenate(
            [
                jnp.concatenate([block((g + h) * GROUP + c) for h in range(2)], axis=1)
                for c in range(GROUP)
            ],
            axis=0,
        )
        for o in range(owners // OCTET):
            out = jnp.dot(pickers[o], right, preferred_element_type=f32)
            for h in range(2):
                part = out[:, h * LANES : (h + 1) * LANES].reshape(OCTET, tall, LANES)
                if (g + h + 1) * GROUP > blocks + 1:
                    first = (blocks + 1 - (g + h) * GROUP) * cap
                    part = jnp.where(last_row >= first, count.astype(f32), part)
                send_ref[
                    o * OCTET : (o + 1) * OCTET, (g + h) * tall : (g + h + 1) * tall, :
                ] = part.astype(bf16)
        part = pl.ds(g * tall, 2 * tall)
        stores.append(pltpu.make_async_copy(send_ref.at[:, part, :], send_hbm.at[:, part, :], store.at[n]))
        stores[-1].start()
    for copy in stores:
        copy.wait()


def policy_kernel(pol_ref, stat_ref):
    slots, columns = pol_ref.shape
    step = 48
    lane = iota((step, LANES), 1)

    def body(i, carry):
        at = pl.ds(pl.multiple_of(i * step, 16), step)
        top = pol_ref[at, 0:LANES].astype(f32)
        for c in range(1, columns // LANES):
            top = jnp.maximum(top, pol_ref[at, c * LANES : (c + 1) * LANES].astype(f32))
        top = jnp.max(top, axis=1, keepdims=True)
        total = jnp.zeros((step, LANES), f32)
        for c in range(columns // LANES):
            total = total + jnp.exp(pol_ref[at, c * LANES : (c + 1) * LANES].astype(f32) - top)
        total = jnp.sum(total, axis=1, keepdims=True)
        stat_ref[at, :] = jnp.where(lane == 0, top, jnp.where(lane == 1, total, 0.0))
        return carry

    lax.fori_loop(0, slots // step, body, 0)


def partial_kernel(cap, got_hbm, pol_ref, stat_ref, rows_ref, part_ref, meta_ref, got_ref, column_ref, load):
    slots, columns = pol_ref.shape
    blocks = columns // LANES
    owners = got_ref.shape[0]
    tall = GROUP * cap
    wide = OCTET * cap
    groups = got_ref.shape[1] // tall
    base = lax.axis_index("tp") * columns
    loads = []
    for o in range(owners // OCTET):
        part = pl.ds(o * OCTET, OCTET)
        loads.append(pltpu.make_async_copy(got_hbm.at[part], got_ref.at[part], load.at[o]))
        loads[-1].start()

    size = OCTET * tall
    a = iota((GROUP, wide, size), 0)
    b = iota((GROUP, wide, size), 1)
    target = b + cap * a
    for d in range(1, OCTET):
        target = target + jnp.where(b >= d * cap, tall - cap, 0)
    order = (target == iota((GROUP, wide, size), 2)).astype(f32).reshape(size, size).astype(bf16)
    lane = iota((wide, LANES), 1)

    for o in range(owners // OCTET):
        at = slice(o * wide, (o + 1) * wide)
        stat = stat_ref[at, :]
        peak = jnp.broadcast_to(stat[:, 0:1], (wide, LANES))
        loads[o].wait()

        def arrived(g):
            pair = [
                got_ref[o * OCTET : (o + 1) * OCTET, (g + h) * tall : (g + h + 1) * tall, :]
                .astype(f32)
                .reshape(size, LANES)
                .astype(bf16)
                for h in range(2)
            ]
            return jnp.dot(order, jnp.concatenate(pair, axis=1), preferred_element_type=f32)

        token = None
        top = jnp.full((wide, LANES), -jnp.inf, f32)
        cross = jnp.zeros((wide, LANES), f32)
        picked = jnp.zeros((wide, LANES), f32)
        info = counts = None
        for g in range(groups - 2, -1, -2):
            product = arrived(g)
            pieces = {
                (g + h) * GROUP + c: product[c * wide : (c + 1) * wide, h * LANES : (h + 1) * LANES]
                for h in range(2)
                for c in range(GROUP)
            }
            if blocks in pieces:
                info, counts = pieces[blocks], pieces[blocks + 1]
                column = (info[:, 0:1] + 256.0 * info[:, 1:2] + 65536.0 * info[:, 2:3]).astype(i32) - base
                token = jnp.broadcast_to(column, (wide, LANES)) - lane
            for c in sorted(n for n in pieces if n < blocks):
                q = pieces[c]
                span = slice(c * LANES, (c + 1) * LANES)
                z = pol_ref[at, span].astype(f32)
                rows_ref[at, span] = q.astype(bf16)
                top = jnp.maximum(top, q)
                cross = cross + jnp.exp(z - peak) * (z - q)
                picked = jnp.where(token == c * LANES, z, picked)
        top = jnp.max(top, axis=1, keepdims=True)
        total = jnp.zeros((wide, LANES), f32)
        for c in range(blocks):
            total = total + jnp.exp(rows_ref[at, c * LANES : (c + 1) * LANES].astype(f32) - top)
        sums = (
            jnp.sum(cross, axis=1, keepdims=True),
            jnp.sum(picked, axis=1, keepdims=True),
            top,
            jnp.sum(total, axis=1, keepdims=True),
            info[:, 3:4],
            info[:, 4:5],
            column.astype(f32),
            counts[:, 0:1],
        )
        out = stat
        for n, value in enumerate(sums):
            out = jnp.where(lane == 2 + n, value, out)
        column_ref[at, :] = out
    column_ref[slots:, :] = jnp.ones((column_ref.shape[0] - slots, LANES), f32)
    turned = column_ref[...].T
    peak, total, cross, picked, top, total_q = (turned[n : n + 1, :] for n in range(6))
    values = (peak + jnp.log(total), cross / total, picked, top + jnp.log(total_q))
    for n, value in enumerate(values):
        part_ref[:, n : n + 1, :] = jnp.broadcast_to(value[None], (part_ref.shape[0],) + value.shape)
    for n in range(4):
        meta_ref[n : n + 1, :] = turned[6 + n : 7 + n, :]
    meta_ref[4:5, :] = peak


def grad_kernel(
    cap, row_total, all_ref, meta_ref, rewards_ref, group_ref, pol_ref, rows_ref, grad_hbm, loss_ref, turn_ref, column_ref, grad_ref, store
):
    slots, columns = pol_ref.shape
    blocks = columns // LANES
    seqs = rewards_ref.shape[0]
    wide = OCTET * cap
    padded = meta_ref.shape[1]

    rewards = rewards_ref[...].reshape(1, seqs)
    groups = group_ref[...].reshape(1, seqs)
    diagonal = iota((seqs, seqs), 0) == iota((seqs, seqs), 1)
    group_down = jnp.sum(jnp.where(diagonal, groups, 0), axis=1, keepdims=True)
    reward_down = jnp.sum(jnp.where(diagonal, rewards, 0.0), axis=1, keepdims=True)
    same = (group_down == groups).astype(f32)
    mean = jnp.sum(same * rewards, axis=1, keepdims=True) / jnp.sum(same, axis=1, keepdims=True)
    advantage = reward_down - mean

    old, tag, token, counts, mine = (meta_ref[n : n + 1, :] for n in range(5))
    valid = tag > 0.5
    adv = jnp.sum(
        jnp.where(iota((seqs, padded), 0) + 1 == tag.astype(i32), advantage, 0.0), axis=0, keepdims=True
    )
    valid_total = jnp.sum(jnp.where(iota((1, padded), 1) < slots, counts, 0.0)) / cap

    logs, gaps, tokens, logs_q = (all_ref[:, n, :] for n in range(4))
    peak = jnp.max(logs, axis=0, keepdims=True)
    weight = jnp.exp(logs - peak)
    total = jnp.sum(weight, axis=0, keepdims=True)
    gap = jnp.sum(gaps * weight, axis=0, keepdims=True) / total
    log_p = peak + jnp.log(total)
    peak_q = jnp.max(logs_q, axis=0, keepdims=True)
    log_q = peak_q + jnp.log(jnp.sum(jnp.exp(logs_q - peak_q), axis=0, keepdims=True))
    kl_term = gap - log_p + log_q
    raw = jnp.sum(tokens, axis=0, keepdims=True) - log_p - old
    ratio = jnp.exp(jnp.clip(raw, -ratio_clamp, ratio_clamp))
    plain = -adv * ratio
    clipped = -adv * jnp.clip(ratio, low_bound, high_bound)
    upper = jnp.maximum(plain, clipped)
    dual = -dual_bound * adv
    negative = adv < 0.0
    loss = jnp.where(negative, jnp.minimum(upper, dual), upper)
    loss_ref[...] = jnp.where(valid, loss + kl_weight * kl_term, 0.0)[:, :slots].reshape(slots)
    inside = (ratio > low_bound) & (ratio < high_bound)
    coef = jnp.where((plain >= clipped) | inside, plain, 0.0)
    coef = jnp.where(negative & (upper > dual), 0.0, coef)
    coef = jnp.where(jnp.abs(raw) < ratio_clamp, coef, 0.0)
    scale = jnp.where(valid, row_total / valid_total, 0.0)
    turn_ref[...] = jnp.zeros(turn_ref.shape, f32)
    share = scale * jnp.exp(mine - peak) / total
    for n, value in enumerate((share * kl_weight, share * coef, scale * coef, gap, token, mine)):
        turn_ref[n : n + 1, :] = value
    column_ref[...] = turn_ref[...].T
    lane = iota((wide, LANES), 1)
    stores = []
    for o in range(slots // wide):
        at = slice(o * wide, (o + 1) * wide)
        slope, level, spike, gaps, col, top = (
            jnp.broadcast_to(column_ref[at, n : n + 1], (wide, LANES)) for n in range(6)
        )
        where = col.astype(i32) - lane
        for c in range(blocks):
            span = slice(c * LANES, (c + 1) * LANES)
            z = pol_ref[at, span].astype(f32)
            q = rows_ref[at, span].astype(f32)
            out = jnp.exp(z - top) * (slope * ((z - q) - gaps) - level)
            out = out + jnp.where(where == c * LANES, spike, 0.0)
            grad_ref[at, span] = out.astype(bf16)
        stores.append(pltpu.make_async_copy(grad_ref.at[at], grad_hbm.at[at], store.at[o]))
        stores[-1].start()
    for copy in stores:
        copy.wait()


def call(kernel, out_shape, ins, outs, scratch=(), cost=None, limit=VMEM_LIMIT):
    spec = {"h": pl.BlockSpec(memory_space=pltpu.HBM), "v": pl.BlockSpec(memory_space=pltpu.VMEM)}
    return pl.pallas_call(
        kernel,
        out_shape=out_shape,
        in_specs=[spec[n] for n in ins],
        out_specs=[spec[n] for n in outs],
        scratch_shapes=list(scratch),
        compiler_params=pltpu.CompilerParams(vmem_limit_bytes=limit),
        cost_estimate=cost,
    )


def shards(ref_logits, token_ids, old_logp, owner_of_row, lengths, rewards, group_ids, pol_logits):
    owners = lax.axis_size("role") * lax.axis_size("dp")
    return steps(owners, ref_logits, token_ids, old_logp, owner_of_row, lengths, rewards, group_ids, pol_logits)


def steps(owners, ref_logits, token_ids, old_logp, owner_of_row, lengths, rewards, group_ids, pol_logits):
    peers = lax.axis_size("tp")
    rows, columns = ref_logits.shape
    slots = pol_logits.shape[0]
    cap = slots // owners
    blocks = columns // LANES
    groups = -(-(blocks + 2) // (2 * GROUP)) * 2
    deep = groups * GROUP * cap
    padded = -(-slots // LANES) * LANES
    shape = jax.ShapeDtypeStruct
    vmem = pltpu.VMEM
    sems = lambda n: pltpu.SemaphoreType.DMA((n,))
    everyone = ("role", "dp")
    octets = owners // OCTET

    [send] = call(
        functools.partial(send_kernel, cap),
        [shape((owners, deep, LANES), bf16)],
        "hhhhh",
        "h",
        (
            vmem((rows,), i32),
            vmem((rows,), bf16),
            vmem((rows,), i32),
            pltpu.SMEM(lengths.shape, i32),
            vmem((rows, columns), bf16),
            vmem((owners, deep, LANES), bf16),
            sems(4),
            sems(groups // 2),
            sems(groups // 2),
        ),
        limit=WHOLE_VMEM,
    )(token_ids, old_logp, owner_of_row, lengths, ref_logits)
    got = lax.all_to_all(send, everyone, split_axis=0, concat_axis=0, tiled=True)
    [stats] = call(
        policy_kernel,
        [shape((slots, LANES), f32)],
        "v",
        "v",
        cost=pl.CostEstimate(
            flops=8 * slots * columns, bytes_accessed=2 * slots * columns, transcendentals=slots * columns
        ),
    )(pol_logits)
    got_rows, parts, meta = call(
        functools.partial(partial_kernel, cap),
        [shape((slots, columns), bf16), shape((peers, 4, padded), f32), shape((8, padded), f32)],
        "hvv",
        "vvv",
        (vmem((owners, deep, LANES), bf16), vmem((padded, LANES), f32), sems(octets)),
    )(got, pol_logits, stats)
    everything = lax.all_to_all(parts, "tp", split_axis=0, concat_axis=0, tiled=True)
    return call(
        functools.partial(grad_kernel, cap, float(rows * owners)),
        [shape((slots, columns), bf16), shape((slots,), f32)],
        "vvvvvv",
        "hv",
        (vmem((LANES, padded), f32), vmem((padded, LANES), f32), vmem((slots, columns), bf16), sems(octets)),
    )(everything, meta, rewards, group_ids, pol_logits, got_rows)


def solution(mesh):
    return jax.shard_map(
        shards,
        mesh=mesh,
        in_specs=(
            P(("role", "dp"), "tp"),
            P(("role", "dp")),
            P(("role", "dp")),
            P(("role", "dp")),
            P(("role", "dp")),
            P(),
            P(),
            P(("role", "dp"), "tp"),
        ),
        out_specs=(P(("role", "dp"), "tp"), P(("role", "dp"))),
        check_vma=False,
    )
```

```python
import functools

import jax
import jax.numpy as jnp
from jax import lax
from jax.experimental import pallas as pl
from jax.experimental.pallas import tpu as pltpu
from jax.sharding import PartitionSpec as P

kl_weight = 0.04
low_bound = 0.8
high_bound = 1.2
dual_bound = 3.0
ratio_clamp = 20.0

LANES = 128
GROUP = 4
OCTET = 8
STORE_ROWS = 16
VMEM_LIMIT = 16 * 1024 * 1024
WHOLE_VMEM = 60 * 1024 * 1024

f32 = jnp.float32
bf16 = jnp.bfloat16
i32 = jnp.int32


def iota(shape, dim):
    return lax.broadcasted_iota(i32, shape, dim)


def send_kernel(
    cap, ids_hbm, old_hbm, owner_hbm, len_hbm, ref_hbm, send_hbm, ids_ref, old_ref, owner_ref, len_ref, ref_ref, send_ref, small, load, store
):
    rows = ref_ref.shape[0]
    blocks = ref_ref.shape[1] // LANES
    owners = send_ref.shape[0]
    tall = GROUP * cap
    groups = send_ref.shape[1] // tall
    seq_local = len_ref.shape[0]
    span = rows // seq_local
    me = lax.axis_index("role") * lax.axis_size("dp") + lax.axis_index("dp")

    smalls = [
        pltpu.make_async_copy(source, target, small.at[n])
        for n, (source, target) in enumerate(
            ((owner_hbm, owner_ref), (ids_hbm, ids_ref), (old_hbm, old_ref), (len_hbm, len_ref))
        )
    ]
    loads = []
    for n, g in enumerate(range(0, groups, 2)):
        part = slice(g * GROUP * LANES, min((g + 2) * GROUP, blocks) * LANES)
        loads.append(pltpu.make_async_copy(ref_hbm.at[:, part], ref_ref.at[:, part], load.at[n]))
    for copy in smalls + loads:
        copy.start()

    before = (iota((rows, rows), 0) < iota((rows, rows), 1)).astype(bf16)
    lane = iota((1, rows), 1)
    feature = iota((LANES, rows), 0)
    smalls[0].wait()
    owner = owner_ref[...].reshape(1, rows)
    hot = (iota((owners, rows), 0) == owner).astype(f32)
    earlier = jnp.dot(hot.astype(bf16), before, preferred_element_type=f32)
    rank = jnp.sum(earlier * hot, axis=0, keepdims=True).astype(i32)
    slot = owner * cap + rank

    for copy in smalls[1:]:
        copy.wait()
    tag = jnp.zeros((1, rows), i32)
    count = jnp.int32(0)
    for s in range(seq_local):
        length = len_ref[s]
        inside = (lane >= s * span) & (lane < s * span + jnp.minimum(length, span))
        tag = jnp.where(inside, me * seq_local + s + 1, tag)
        count = count + jnp.clip(length, 0, span)
    ids = ids_ref[...].reshape(1, rows)
    table = jnp.zeros((LANES, rows), f32)
    values = (
        (ids & 255).astype(f32),
        ((ids >> 8) & 255).astype(f32),
        (ids >> 16).astype(f32),
        old_ref[...].reshape(1, rows).astype(f32),
        tag.astype(f32),
    )
    for n, value in enumerate(values):
        table = jnp.where(feature == n, value, table)
    table = table.T
    column = iota((rows, LANES), 1)
    nothing = jnp.zeros((rows, LANES), bf16)

    def block(c):
        if c < blocks:
            return ref_ref[:, c * LANES : (c + 1) * LANES]
        return table if c == blocks else nothing

    half = tall - 8
    row = iota((OCTET, half, rows), 1)
    place = iota((OCTET, half, rows), 0) * cap + row
    pickers = []
    for o in range(owners // OCTET):
        for side in range(2):
            parts = []
            for c in range(2 * side, 2 * side + 2):
                first = c * cap - 8 * side
                mine = (row >= first) & (row < first + cap)
                hit = mine & (place + (o * OCTET * cap - first) == slot.reshape(1, 1, rows))
                parts.append(hit.astype(f32).reshape(OCTET * half, rows).astype(bf16))
            pickers.append(jnp.concatenate(parts, axis=1))
    last_row = iota((OCTET, tall, LANES), 1)
    highest = None
    stores = []
    for n, g in enumerate(range(0, groups, 2)):
        loads[n].wait()
        for c in range(g * GROUP, min((g + 2) * GROUP, blocks)):
            highest = block(c) if highest is None else jnp.maximum(highest, block(c))
        if (g + 2) * GROUP > blocks:
            table = jnp.where(column == len(values), jnp.max(highest.astype(f32), axis=1, keepdims=True), table).astype(bf16)
        right = [
            jnp.concatenate(
                [
                    jnp.concatenate([block((g + h) * GROUP + 2 * side + c) for h in range(2)], axis=1)
                    for c in range(2)
                ],
                axis=0,
            )
            for side in range(2)
        ]
        for o in range(owners // OCTET):
            out = [
                jnp.dot(pickers[2 * o + side], right[side], preferred_element_type=f32).reshape(OCTET, half, 2 * LANES)
                for side in range(2)
            ]
            both = jnp.concatenate([out[0][:, 0:8], out[0][:, 8:] + out[1][:, : half - 8], out[1][:, half - 8 :]], axis=1)
            for h in range(2):
                part = both[:, :, h * LANES : (h + 1) * LANES]
                if (g + h + 1) * GROUP > blocks + 1:
                    first = (blocks + 1 - (g + h) * GROUP) * cap
                    part = jnp.where(last_row >= first, count.astype(f32), part)
                send_ref[
                    o * OCTET : (o + 1) * OCTET, (g + h) * tall : (g + h + 1) * tall, :
                ] = part.astype(bf16)
        part = pl.ds(g * tall, 2 * tall)
        stores.append(pltpu.make_async_copy(send_ref.at[:, part, :], send_hbm.at[:, part, :], store.at[n]))
        stores[-1].start()
    for copy in stores:
        copy.wait()


def partial_kernel(cap, got_ref, pol_ref, exp_ref, gap_ref, part_ref, meta_ref, column_ref):
    slots, columns = pol_ref.shape
    blocks = columns // LANES
    owners = got_ref.shape[0]
    tall = GROUP * cap
    wide = OCTET * cap
    groups = got_ref.shape[1] // tall
    base = lax.axis_index("tp") * columns

    size = OCTET * tall
    a = iota((GROUP, wide, size), 0)
    b = iota((GROUP, wide, size), 1)
    target = b + cap * a
    for d in range(1, OCTET):
        target = target + jnp.where(b >= d * cap, tall - cap, 0)
    order = (target == iota((GROUP, wide, size), 2)).astype(f32).reshape(size, size).astype(bf16)
    lane = iota((wide, LANES), 1)

    for o in range(owners // OCTET):
        at = slice(o * wide, (o + 1) * wide)
        highest = pol_ref[at, 0:LANES]
        for c in range(1, blocks):
            highest = jnp.maximum(highest, pol_ref[at, c * LANES : (c + 1) * LANES])
        peak = jnp.max(highest.astype(f32), axis=1, keepdims=True)
        peaks = jnp.broadcast_to(peak, (wide, LANES))

        def arrived(g):
            pair = [
                got_ref[o * OCTET : (o + 1) * OCTET, (g + h) * tall : (g + h + 1) * tall, :]
                .astype(f32)
                .reshape(size, LANES)
                .astype(bf16)
                for h in range(2)
            ]
            return jnp.dot(order, jnp.concatenate(pair, axis=1), preferred_element_type=f32)

        token = None
        total, cross, picked, total_q = (jnp.zeros((wide, LANES), f32) for _ in range(4))
        info = counts = None
        for g in range(groups - 2, -1, -2):
            product = arrived(g)
            pieces = {
                (g + h) * GROUP + c: product[c * wide : (c + 1) * wide, h * LANES : (h + 1) * LANES]
                for h in range(2)
                for c in range(GROUP)
            }
            if blocks in pieces:
                info, counts = pieces[blocks], pieces[blocks + 1]
                column = (info[:, 0:1] + 256.0 * info[:, 1:2] + 65536.0 * info[:, 2:3]).astype(i32) - base
                token = jnp.broadcast_to(column, (wide, LANES)) - lane
                top = info[:, 5:6]
                tops = jnp.broadcast_to(top, (wide, LANES))
            for c in sorted(n for n in pieces if n < blocks):
                q = pieces[c]
                span = slice(c * LANES, (c + 1) * LANES)
                z = pol_ref[at, span].astype(f32)
                exps = jnp.exp(z - peaks)
                gaps = exps * (z - q)
                exp_ref[at, span] = exps
                gap_ref[at, span] = gaps
                total = total + exps
                cross = cross + gaps
                total_q = total_q + jnp.exp(q - tops)
                picked = jnp.where(token == c * LANES, z, picked)
        sums = (
            peak,
            jnp.sum(total, axis=1, keepdims=True),
            jnp.sum(cross, axis=1, keepdims=True),
            jnp.sum(picked, axis=1, keepdims=True),
            top,
            jnp.sum(total_q, axis=1, keepdims=True),
            info[:, 3:4],
            info[:, 4:5],
            column.astype(f32),
            counts[:, 0:1],
        )
        out = jnp.zeros((wide, LANES), f32)
        for n, value in enumerate(sums):
            out = jnp.where(lane == n, value, out)
        column_ref[at, :] = out
    column_ref[slots:, :] = jnp.ones((column_ref.shape[0] - slots, LANES), f32)
    turned = column_ref[...].T
    peak, total, cross, picked, top, total_q = (turned[n : n + 1, :] for n in range(6))
    values = (peak + jnp.log(total), cross / total, picked, top + jnp.log(total_q))
    for n, value in enumerate(values):
        part_ref[:, n : n + 1, :] = jnp.broadcast_to(value[None], (part_ref.shape[0],) + value.shape)
    for n in range(4):
        meta_ref[n : n + 1, :] = turned[6 + n : 7 + n, :]
    meta_ref[4:5, :] = peak


def grad_kernel(
    cap, row_total, all_ref, meta_ref, rewards_ref, group_ref, exp_ref, gap_ref, grad_hbm, loss_ref, turn_ref, column_ref, grad_ref, store
):
    slots, columns = exp_ref.shape
    blocks = columns // LANES
    seqs = rewards_ref.shape[0]
    padded = meta_ref.shape[1]

    rewards = rewards_ref[...].reshape(1, seqs)
    groups = group_ref[...].reshape(1, seqs)
    diagonal = iota((seqs, seqs), 0) == iota((seqs, seqs), 1)
    group_down = jnp.sum(jnp.where(diagonal, groups, 0), axis=1, keepdims=True)
    reward_down = jnp.sum(jnp.where(diagonal, rewards, 0.0), axis=1, keepdims=True)
    same = (group_down == groups).astype(f32)
    mean = jnp.sum(same * rewards, axis=1, keepdims=True) / jnp.sum(same, axis=1, keepdims=True)
    advantage = reward_down - mean

    old, tag, token, counts, mine = (meta_ref[n : n + 1, :] for n in range(5))
    valid = tag > 0.5
    adv = jnp.sum(
        jnp.where(iota((seqs, padded), 0) + 1 == tag.astype(i32), advantage, 0.0), axis=0, keepdims=True
    )
    valid_total = jnp.sum(jnp.where(iota((1, padded), 1) < slots, counts, 0.0)) / cap

    logs, gaps, tokens, logs_q = (all_ref[:, n, :] for n in range(4))
    peak = jnp.max(logs, axis=0, keepdims=True)
    weight = jnp.exp(logs - peak)
    total = jnp.sum(weight, axis=0, keepdims=True)
    gap = jnp.sum(gaps * weight, axis=0, keepdims=True) / total
    log_p = peak + jnp.log(total)
    peak_q = jnp.max(logs_q, axis=0, keepdims=True)
    log_q = peak_q + jnp.log(jnp.sum(jnp.exp(logs_q - peak_q), axis=0, keepdims=True))
    kl_term = gap - log_p + log_q
    raw = jnp.sum(tokens, axis=0, keepdims=True) - log_p - old
    ratio = jnp.exp(jnp.clip(raw, -ratio_clamp, ratio_clamp))
    plain = -adv * ratio
    clipped = -adv * jnp.clip(ratio, low_bound, high_bound)
    upper = jnp.maximum(plain, clipped)
    dual = -dual_bound * adv
    negative = adv < 0.0
    loss = jnp.where(negative, jnp.minimum(upper, dual), upper)
    loss_ref[...] = jnp.where(valid, loss + kl_weight * kl_term, 0.0)[:, :slots].reshape(slots)
    inside = (ratio > low_bound) & (ratio < high_bound)
    coef = jnp.where((plain >= clipped) | inside, plain, 0.0)
    coef = jnp.where(negative & (upper > dual), 0.0, coef)
    coef = jnp.where(jnp.abs(raw) < ratio_clamp, coef, 0.0)
    scale = jnp.where(valid, row_total / valid_total, 0.0)
    turn_ref[...] = jnp.zeros(turn_ref.shape, f32)
    share = scale * jnp.exp(mine - peak) / total
    slope = share * kl_weight
    for n, value in enumerate((slope, slope * gap + share * coef, scale * coef, token)):
        turn_ref[n : n + 1, :] = value
    column_ref[...] = turn_ref[...].T
    step = slots // store.shape[0]
    lane = iota((step, LANES), 1)
    stores = []
    for i in range(slots // step):
        at = slice(i * step, (i + 1) * step)
        slope, level, spike, col = (
            jnp.broadcast_to(column_ref[at, n : n + 1], (step, LANES)) for n in range(4)
        )
        where = col.astype(i32) - lane
        for c in range(blocks):
            span = slice(c * LANES, (c + 1) * LANES)
            out = slope * gap_ref[at, span] - level * exp_ref[at, span]
            out = out + jnp.where(where == c * LANES, spike, 0.0)
            grad_ref[at, span] = out.astype(bf16)
        stores.append(pltpu.make_async_copy(grad_ref.at[at], grad_hbm.at[at], store.at[i]))
        stores[-1].start()
    for copy in stores:
        copy.wait()


def call(kernel, out_shape, ins, outs, scratch=(), cost=None, limit=VMEM_LIMIT):
    spec = {"h": pl.BlockSpec(memory_space=pltpu.HBM), "v": pl.BlockSpec(memory_space=pltpu.VMEM)}
    return pl.pallas_call(
        kernel,
        out_shape=out_shape,
        in_specs=[spec[n] for n in ins],
        out_specs=[spec[n] for n in outs],
        scratch_shapes=list(scratch),
        compiler_params=pltpu.CompilerParams(vmem_limit_bytes=limit),
        cost_estimate=cost,
    )


def shards(ref_logits, token_ids, old_logp, owner_of_row, lengths, rewards, group_ids, pol_logits):
    owners = lax.axis_size("role") * lax.axis_size("dp")
    return steps(owners, ref_logits, token_ids, old_logp, owner_of_row, lengths, rewards, group_ids, pol_logits)


def steps(owners, ref_logits, token_ids, old_logp, owner_of_row, lengths, rewards, group_ids, pol_logits):
    peers = lax.axis_size("tp")
    rows, columns = ref_logits.shape
    slots = pol_logits.shape[0]
    cap = slots // owners
    blocks = columns // LANES
    groups = -(-(blocks + 2) // (2 * GROUP)) * 2
    deep = groups * GROUP * cap
    padded = -(-slots // LANES) * LANES
    shape = jax.ShapeDtypeStruct
    vmem = pltpu.VMEM
    sems = lambda n: pltpu.SemaphoreType.DMA((n,))
    everyone = ("role", "dp")

    [send] = call(
        functools.partial(send_kernel, cap),
        [shape((owners, deep, LANES), bf16)],
        "hhhhh",
        "h",
        (
            vmem((rows,), i32),
            vmem((rows,), bf16),
            vmem((rows,), i32),
            pltpu.SMEM(lengths.shape, i32),
            vmem((rows, columns), bf16),
            vmem((owners, deep, LANES), bf16),
            sems(4),
            sems(groups // 2),
            sems(groups // 2),
        ),
        limit=WHOLE_VMEM,
    )(token_ids, old_logp, owner_of_row, lengths, ref_logits)
    got = lax.all_to_all(send, everyone, split_axis=0, concat_axis=0, tiled=True)
    exps, gaps, parts, meta = call(
        functools.partial(partial_kernel, cap),
        [
            shape((slots, columns), f32),
            shape((slots, columns), f32),
            shape((peers, 4, padded), f32),
            shape((8, padded), f32),
        ],
        "vv",
        "vvvv",
        (vmem((padded, LANES), f32),),
    )(got, pol_logits)
    everything = lax.all_to_all(parts, "tp", split_axis=0, concat_axis=0, tiled=True)
    pieces = slots // STORE_ROWS
    return call(
        functools.partial(grad_kernel, cap, float(rows * owners)),
        [shape((slots, columns), bf16), shape((slots,), f32)],
        "vvvvvv",
        "hv",
        (vmem((LANES, padded), f32), vmem((padded, LANES), f32), vmem((slots, columns), bf16), sems(pieces)),
    )(everything, meta, rewards, group_ids, exps, gaps)


def solution(mesh):
    return jax.shard_map(
        shards,
        mesh=mesh,
        in_specs=(
            P(("role", "dp"), "tp"),
            P(("role", "dp")),
            P(("role", "dp")),
            P(("role", "dp")),
            P(("role", "dp")),
            P(),
            P(),
            P(("role", "dp"), "tp"),
        ),
        out_specs=(P(("role", "dp"), "tp"), P(("role", "dp"))),
        check_vma=False,
    )
```

```python
import functools

import jax
import jax.numpy as jnp
from jax import lax
from jax.experimental import pallas as pl
from jax.experimental.pallas import tpu as pltpu
from jax.sharding import PartitionSpec as P

kl_weight = 0.04
low_bound = 0.8
high_bound = 1.2
dual_bound = 3.0
ratio_clamp = 20.0

LANES = 128
GROUP = 4
HALF = 64
OCTET = 8
STORE_ROWS = 16
VMEM_LIMIT = 16 * 1024 * 1024

f32 = jnp.float32
bf16 = jnp.bfloat16
i32 = jnp.int32


def iota(shape, dim):
    return lax.broadcasted_iota(i32, shape, dim)


def send_kernel(
    cap, ids_hbm, old_hbm, owner_hbm, len_hbm, ref_hbm, send_ref, ids_ref, old_ref, owner_ref, len_ref, ref_ref, small, load
):
    rows = ref_ref.shape[0]
    blocks = ref_ref.shape[1] // LANES
    owners = send_ref.shape[0]
    tall = GROUP * cap
    full = blocks // GROUP
    seq_local = len_ref.shape[0]
    span = rows // seq_local
    me = lax.axis_index("role") * lax.axis_size("dp") + lax.axis_index("dp")

    smalls = [
        pltpu.make_async_copy(source, target, small.at[n])
        for n, (source, target) in enumerate(
            ((owner_hbm, owner_ref), (ids_hbm, ids_ref), (old_hbm, old_ref), (len_hbm, len_ref))
        )
    ]
    loads = []
    for n, g in enumerate(range(0, full, 2)):
        part = slice(g * GROUP * LANES, min((g + 2) * GROUP, blocks) * LANES)
        loads.append(pltpu.make_async_copy(ref_hbm.at[:, part], ref_ref.at[:, part], load.at[n]))
    for copy in smalls + loads:
        copy.start()

    before = (iota((rows, rows), 0) < iota((rows, rows), 1)).astype(bf16)
    lane = iota((1, rows), 1)
    feature = iota((LANES, rows), 0)
    smalls[0].wait()
    owner = owner_ref[...].reshape(1, rows)
    hot = (iota((owners, rows), 0) == owner).astype(f32)
    earlier = jnp.dot(hot.astype(bf16), before, preferred_element_type=f32)
    rank = jnp.sum(earlier * hot, axis=0, keepdims=True).astype(i32)
    slot = owner * cap + rank

    for copy in smalls[1:]:
        copy.wait()
    tag = jnp.zeros((1, rows), i32)
    count = jnp.int32(0)
    for s in range(seq_local):
        length = len_ref[s]
        inside = (lane >= s * span) & (lane < s * span + jnp.minimum(length, span))
        tag = jnp.where(inside, me * seq_local + s + 1, tag)
        count = count + jnp.clip(length, 0, span)
    ids = ids_ref[...].reshape(1, rows)
    table = jnp.zeros((LANES, rows), f32)
    values = (
        (ids & 255).astype(f32),
        ((ids >> 8) & 255).astype(f32),
        (ids >> 16).astype(f32),
        old_ref[...].reshape(1, rows).astype(f32),
        tag.astype(f32),
        jnp.ones((1, rows), f32),
    )
    place_of = feature - (slot & 1) * HALF
    for n, value in enumerate(values):
        table = jnp.where(place_of == n, value, table)
    table = table.T
    column = iota((rows, LANES), 1) & (HALF - 1)
    nothing = jnp.zeros((rows, LANES), bf16)

    def block(c):
        return ref_ref[:, c * LANES : (c + 1) * LANES] if c < blocks else nothing

    half = tall - 8
    row = iota((OCTET, half, rows), 1)
    place = iota((OCTET, half, rows), 0) * cap + row
    pickers = []
    for o in range(owners // OCTET):
        for side in range(2):
            parts = []
            for c in range(2 * side, 2 * side + 2):
                first = c * cap - 8 * side
                mine = (row >= first) & (row < first + cap)
                hit = mine & (place + (o * OCTET * cap - first) == slot.reshape(1, 1, rows))
                parts.append(hit.astype(f32).reshape(OCTET * half, rows).astype(bf16))
            pickers.append(jnp.concatenate(parts, axis=1))
    last_row = iota((OCTET, half, LANES), 1)
    highest = None
    tails = []
    for n, g in enumerate(range(0, full, 2)):
        loads[n].wait()
        for c in range(g * GROUP, min((g + 2) * GROUP, blocks)):
            highest = block(c) if highest is None else jnp.maximum(highest, block(c))
        right = [
            jnp.concatenate(
                [
                    jnp.concatenate([block((g + h) * GROUP + 2 * side + c) for h in range(2)], axis=1)
                    for c in range(2)
                ],
                axis=0,
            )
            for side in range(2)
        ]
        for o in range(owners // OCTET):
            out = [
                jnp.dot(pickers[2 * o + side], right[side], preferred_element_type=f32).reshape(OCTET, half, 2 * LANES)
                for side in range(2)
            ]
            both = jnp.concatenate([out[0][:, 0:8], out[0][:, 8:] + out[1][:, : half - 8], out[1][:, half - 8 :]], axis=1)
            for h in range(min(2, full - g)):
                send_ref[o * OCTET : (o + 1) * OCTET, (g + h) * tall : (g + h + 1) * tall, :] = both[
                    :, :, h * LANES : (h + 1) * LANES
                ].astype(bf16)
            if g + 2 > full:
                tails.append(out[0][:, :, LANES:])
    top = jnp.max(highest.astype(f32), axis=1, keepdims=True)
    table = jnp.where(column == len(values) - 1, table * top, table).astype(bf16)
    for o in range(owners // OCTET):
        pair = iota((OCTET, half, rows), 0) * (cap // 2) + row + (o * OCTET * (cap // 2) - 2 * cap)
        hit = (row >= 2 * cap) & (row < half - 1) & (pair == (slot >> 1).reshape(1, 1, rows))
        picker = hit.astype(f32).reshape(OCTET * half, rows).astype(bf16)
        extra = jnp.dot(picker, table, preferred_element_type=f32).reshape(OCTET, half, LANES)
        tail = jnp.where(last_row == half - 1, count.astype(f32), tails[o] + extra)
        send_ref[o * OCTET : (o + 1) * OCTET, full * tall :, :] = tail.astype(bf16)


def partial_kernel(cap, got_ref, pol_ref, exp_ref, gap_ref, part_ref, meta_ref, column_ref):
    slots, columns = pol_ref.shape
    blocks = columns // LANES
    owners = got_ref.shape[0]
    tall = GROUP * cap
    wide = OCTET * cap
    full = blocks // GROUP
    half = tall - 8
    base = lax.axis_index("tp") * columns

    size = OCTET * tall
    a = iota((GROUP, wide, size), 0)
    b = iota((GROUP, wide, size), 1)
    target = b + cap * a
    for d in range(1, OCTET):
        target = target + jnp.where(b >= d * cap, tall - cap, 0)
    order = (target == iota((GROUP, wide, size), 2)).astype(f32).reshape(size, size).astype(bf16)
    small = OCTET * half
    a = iota((3, wide, small), 0)
    b = iota((3, wide, small), 1)
    slot_row = b
    source = jnp.zeros_like(b)
    for d in range(1, OCTET):
        slot_row = slot_row - jnp.where(b >= d * cap, cap, 0)
        source = source + jnp.where(b >= d * cap, half, 0)
    source = source + jnp.where(a == 2, 2 * cap + (slot_row >> 1), a * cap + slot_row)
    tail_order = (source == iota((3, wide, small), 2)).astype(f32).reshape(3 * wide, small).astype(bf16)
    lane = iota((wide, LANES), 1)
    odd = (iota((wide, LANES), 0) & 1) == 1
    counts = jnp.zeros((1, LANES), f32)

    for o in range(owners // OCTET):
        at = slice(o * wide, (o + 1) * wide)
        highest = pol_ref[at, 0:LANES]
        for c in range(1, blocks):
            highest = jnp.maximum(highest, pol_ref[at, c * LANES : (c + 1) * LANES])
        peak = jnp.max(highest.astype(f32), axis=1, keepdims=True)
        peaks = jnp.broadcast_to(peak, (wide, LANES))

        def arrived(first, rows, ways, matrix):
            parts = [
                got_ref[o * OCTET : (o + 1) * OCTET, first + h * rows : first + (h + 1) * rows, :]
                .astype(f32)
                .reshape(OCTET * rows, LANES)
                .astype(bf16)
                for h in range(ways)
            ]
            right = jnp.concatenate(parts, axis=1) if ways > 1 else parts[0]
            return jnp.dot(matrix, right, preferred_element_type=f32)

        product = arrived(full * tall, half, 1, tail_order)
        todo = [{full * GROUP + c: product[c * wide : (c + 1) * wide] for c in range(2)}]
        info = product[2 * wide :]
        info = jnp.where(odd, pltpu.roll(info, HALF, 1), info)
        last = got_ref[o * OCTET : (o + 1) * OCTET, full * tall + 8 :, :].astype(f32)
        counts = counts + jnp.sum(last[:, half - 9, :], axis=0, keepdims=True)
        column = (info[:, 0:1] + 256.0 * info[:, 1:2] + 65536.0 * info[:, 2:3]).astype(i32) - base
        token = jnp.broadcast_to(column, (wide, LANES)) - lane
        top = info[:, 5:6]
        tops = jnp.broadcast_to(top, (wide, LANES))
        total, cross, picked, total_q = (jnp.zeros((wide, LANES), f32) for _ in range(4))
        for g in range(full - 1, -1, -2):
            ways = 2 if g else 1
            product = arrived((g - ways + 1) * tall, tall, ways, order)
            todo.append(
                {
                    (g - ways + 1 + h) * GROUP + c: product[c * wide : (c + 1) * wide, h * LANES : (h + 1) * LANES]
                    for h in range(ways)
                    for c in range(GROUP)
                }
            )
        for pieces in todo:
            for c in sorted(pieces):
                q = pieces[c]
                span = slice(c * LANES, (c + 1) * LANES)
                z = pol_ref[at, span].astype(f32)
                exps = jnp.exp(z - peaks)
                gaps = exps * (z - q)
                exp_ref[at, span] = exps
                gap_ref[at, span] = gaps
                total = total + exps
                cross = cross + gaps
                total_q = total_q + jnp.exp(q - tops)
                picked = jnp.where(token == c * LANES, z, picked)
        sums = (
            peak,
            jnp.sum(total, axis=1, keepdims=True),
            jnp.sum(cross, axis=1, keepdims=True),
            jnp.sum(picked, axis=1, keepdims=True),
            top,
            jnp.sum(total_q, axis=1, keepdims=True),
            info[:, 3:4],
            info[:, 4:5],
            column.astype(f32),
        )
        out = jnp.zeros((wide, LANES), f32)
        for n, value in enumerate(sums):
            out = jnp.where(lane == n, value, out)
        column_ref[at, :] = out
    column_ref[slots:, :] = jnp.ones((column_ref.shape[0] - slots, LANES), f32)
    turned = column_ref[...].T
    peak, total, cross, picked, top, total_q = (turned[n : n + 1, :] for n in range(6))
    pairs = ((peak + jnp.log(total), cross / total), (picked, top + jnp.log(total_q)))
    for n, pair in enumerate(pairs):
        line = jnp.concatenate([value[:, :slots] for value in pair], axis=1)
        part_ref[:, n : n + 1, :] = jnp.broadcast_to(line[None], (part_ref.shape[0],) + line.shape)
    for n in range(3):
        meta_ref[n : n + 1, :] = turned[6 + n : 7 + n, :]
    meta_ref[3:4, :] = jnp.concatenate([counts] * (meta_ref.shape[1] // LANES), axis=1)
    meta_ref[4:5, :] = peak


def grad_kernel(
    row_total, all_ref, meta_ref, rewards_ref, group_ref, exp_ref, gap_ref, grad_hbm, loss_ref, turn_ref, column_ref, grad_ref, store
):
    slots, columns = exp_ref.shape
    blocks = columns // LANES
    seqs = rewards_ref.shape[0]

    rewards = rewards_ref[...].reshape(1, seqs)
    groups = group_ref[...].reshape(1, seqs)
    diagonal = iota((seqs, seqs), 0) == iota((seqs, seqs), 1)
    group_down = jnp.sum(jnp.where(diagonal, groups, 0), axis=1, keepdims=True)
    reward_down = jnp.sum(jnp.where(diagonal, rewards, 0.0), axis=1, keepdims=True)
    same = (group_down == groups).astype(f32)
    mean = jnp.sum(same * rewards, axis=1, keepdims=True) / jnp.sum(same, axis=1, keepdims=True)
    advantage = reward_down - mean

    old, tag, token, valid_total, mine = (meta_ref[n : n + 1, :slots] for n in range(5))
    valid = tag > 0.5
    adv = jnp.sum(
        jnp.where(iota((seqs, slots), 0) + 1 == tag.astype(i32), advantage, 0.0), axis=0, keepdims=True
    )

    logs, gaps, tokens, logs_q = (all_ref[:, n, m * slots : (m + 1) * slots] for n in range(2) for m in range(2))
    peak = jnp.max(logs, axis=0, keepdims=True)
    weight = jnp.exp(logs - peak)
    total = jnp.sum(weight, axis=0, keepdims=True)
    gap = jnp.sum(gaps * weight, axis=0, keepdims=True) / total
    log_p = peak + jnp.log(total)
    peak_q = jnp.max(logs_q, axis=0, keepdims=True)
    log_q = peak_q + jnp.log(jnp.sum(jnp.exp(logs_q - peak_q), axis=0, keepdims=True))
    kl_term = gap - log_p + log_q
    raw = jnp.sum(tokens, axis=0, keepdims=True) - log_p - old
    ratio = jnp.exp(jnp.clip(raw, -ratio_clamp, ratio_clamp))
    plain = -adv * ratio
    clipped = -adv * jnp.clip(ratio, low_bound, high_bound)
    upper = jnp.maximum(plain, clipped)
    dual = -dual_bound * adv
    negative = adv < 0.0
    loss = jnp.where(negative, jnp.minimum(upper, dual), upper)
    loss_ref[...] = jnp.where(valid, loss + kl_weight * kl_term, 0.0).reshape(slots)
    inside = (ratio > low_bound) & (ratio < high_bound)
    coef = jnp.where((plain >= clipped) | inside, plain, 0.0)
    coef = jnp.where(negative & (upper > dual), 0.0, coef)
    coef = jnp.where(jnp.abs(raw) < ratio_clamp, coef, 0.0)
    scale = jnp.where(valid, row_total / valid_total, 0.0)
    turn_ref[...] = jnp.zeros(turn_ref.shape, f32)
    share = scale * jnp.exp(mine - peak) / total
    slope = share * kl_weight
    for n, value in enumerate((slope, slope * gap + share * coef, scale * coef, token)):
        turn_ref[n : n + 1, :slots] = value
    column_ref[...] = turn_ref[...].T
    step = slots // store.shape[0]
    lane = iota((step, LANES), 1)
    stores = []
    for i in range(slots // step):
        at = slice(i * step, (i + 1) * step)
        slope, level, spike, col = (
            jnp.broadcast_to(column_ref[at, n : n + 1], (step, LANES)) for n in range(4)
        )
        where = col.astype(i32) - lane
        for c in range(blocks):
            span = slice(c * LANES, (c + 1) * LANES)
            out = slope * gap_ref[at, span] - level * exp_ref[at, span]
            out = out + jnp.where(where == c * LANES, spike, 0.0)
            grad_ref[at, span] = out.astype(bf16)
        stores.append(pltpu.make_async_copy(grad_ref.at[at], grad_hbm.at[at], store.at[i]))
        stores[-1].start()
    for copy in stores:
        copy.wait()


def call(kernel, out_shape, ins, outs, scratch=(), cost=None, limit=VMEM_LIMIT):
    spec = {"h": pl.BlockSpec(memory_space=pltpu.HBM), "v": pl.BlockSpec(memory_space=pltpu.VMEM)}
    return pl.pallas_call(
        kernel,
        out_shape=out_shape,
        in_specs=[spec[n] for n in ins],
        out_specs=[spec[n] for n in outs],
        scratch_shapes=list(scratch),
        compiler_params=pltpu.CompilerParams(vmem_limit_bytes=limit),
        cost_estimate=cost,
    )


def shards(ref_logits, token_ids, old_logp, owner_of_row, lengths, rewards, group_ids, pol_logits):
    owners = lax.axis_size("role") * lax.axis_size("dp")
    return steps(owners, ref_logits, token_ids, old_logp, owner_of_row, lengths, rewards, group_ids, pol_logits)


def steps(owners, ref_logits, token_ids, old_logp, owner_of_row, lengths, rewards, group_ids, pol_logits):
    peers = lax.axis_size("tp")
    rows, columns = ref_logits.shape
    slots = pol_logits.shape[0]
    cap = slots // owners
    blocks = columns // LANES
    full = blocks // GROUP
    deep = blocks * cap + 4
    padded = -(-slots // LANES) * LANES
    shape = jax.ShapeDtypeStruct
    vmem = pltpu.VMEM
    sems = lambda n: pltpu.SemaphoreType.DMA((n,))
    everyone = ("role", "dp")

    [send] = call(
        functools.partial(send_kernel, cap),
        [shape((owners, deep, LANES), bf16)],
        "hhhhh",
        "v",
        (
            vmem((rows,), i32),
            vmem((rows,), bf16),
            vmem((rows,), i32),
            pltpu.SMEM(lengths.shape, i32),
            vmem((rows, columns), bf16),
            sems(4),
            sems(full // 2 + 1),
        ),
        limit=VMEM_LIMIT,
    )(*(pltpu.with_memory_space_constraint(x, pltpu.HBM) for x in (token_ids, old_logp, owner_of_row, lengths, ref_logits)))
    got = lax.all_to_all(send, everyone, split_axis=0, concat_axis=0, tiled=True)
    exps, gaps, parts, meta = call(
        functools.partial(partial_kernel, cap),
        [
            shape((slots, columns), f32),
            shape((slots, columns), f32),
            shape((peers, 2, 2 * slots), f32),
            shape((8, padded), f32),
        ],
        "vv",
        "vvvv",
        (vmem((padded, LANES), f32),),
    )(got, pol_logits)
    everything = lax.all_to_all(parts, "tp", split_axis=0, concat_axis=0, tiled=True)
    pieces = slots // STORE_ROWS
    return call(
        functools.partial(grad_kernel, float(rows * owners)),
        [shape((slots, columns), bf16), shape((slots,), f32)],
        "vvvvvv",
        "hv",
        (vmem((LANES, padded), f32), vmem((padded, LANES), f32), vmem((slots, columns), bf16), sems(pieces)),
    )(everything, meta, rewards, group_ids, exps, gaps)


def solution(mesh):
    return jax.shard_map(
        shards,
        mesh=mesh,
        in_specs=(
            P(("role", "dp"), "tp"),
            P(("role", "dp")),
            P(("role", "dp")),
            P(("role", "dp")),
            P(("role", "dp")),
            P(),
            P(),
            P(("role", "dp"), "tp"),
        ),
        out_specs=(P(("role", "dp"), "tp"), P(("role", "dp"))),
        check_vma=False,
    )
```

```python
import functools

import jax
import jax.numpy as jnp
from jax import lax
from jax.experimental import pallas as pl
from jax.experimental.pallas import tpu as pltpu
from jax.sharding import PartitionSpec as P

kl_weight = 0.04
low_bound = 0.8
high_bound = 1.2
dual_bound = 3.0
ratio_clamp = 20.0

LANES = 128
GROUP = 4
HALF = 64
OCTET = 8
STORE_ROWS = 16
VMEM_LIMIT = 16 * 1024 * 1024

f32 = jnp.float32
bf16 = jnp.bfloat16
i32 = jnp.int32


def iota(shape, dim):
    return lax.broadcasted_iota(i32, shape, dim)


def send_kernel(
    cap, ids_hbm, old_hbm, owner_hbm, len_hbm, ref_hbm, send_ref, ids_ref, old_ref, owner_ref, len_ref, ref_ref, small, load
):
    rows = ref_ref.shape[0]
    blocks = ref_ref.shape[1] // LANES
    owners = send_ref.shape[0]
    tall = GROUP * cap
    full = blocks // GROUP
    seq_local = len_ref.shape[0]
    span = rows // seq_local
    me = lax.axis_index("role") * lax.axis_size("dp") + lax.axis_index("dp")

    smalls = [
        pltpu.make_async_copy(source, target, small.at[n])
        for n, (source, target) in enumerate(
            ((owner_hbm, owner_ref), (ids_hbm, ids_ref), (old_hbm, old_ref), (len_hbm, len_ref))
        )
    ]
    loads = []
    for n, g in enumerate(range(0, full, 2)):
        part = slice(g * GROUP * LANES, min((g + 2) * GROUP, blocks) * LANES)
        loads.append(pltpu.make_async_copy(ref_hbm.at[:, part], ref_ref.at[:, part], load.at[n]))
    for copy in smalls + loads:
        copy.start()

    before = (iota((rows, rows), 0) < iota((rows, rows), 1)).astype(bf16)
    lane = iota((1, rows), 1)
    feature = iota((LANES, rows), 0)
    smalls[0].wait()
    owner = owner_ref[...].reshape(1, rows)
    hot = (iota((owners, rows), 0) == owner).astype(f32)
    earlier = jnp.dot(hot.astype(bf16), before, preferred_element_type=f32)
    rank = jnp.sum(earlier * hot, axis=0, keepdims=True).astype(i32)
    slot = owner * cap + rank

    for copy in smalls[1:]:
        copy.wait()
    tag = jnp.zeros((1, rows), i32)
    count = jnp.int32(0)
    for s in range(seq_local):
        length = len_ref[s]
        inside = (lane >= s * span) & (lane < s * span + jnp.minimum(length, span))
        tag = jnp.where(inside, me * seq_local + s + 1, tag)
        count = count + jnp.clip(length, 0, span)
    ids = ids_ref[...].reshape(1, rows)
    table = jnp.zeros((LANES, rows), f32)
    values = (
        (ids & 255).astype(f32),
        ((ids >> 8) & 255).astype(f32),
        (ids >> 16).astype(f32),
        old_ref[...].reshape(1, rows).astype(f32),
        tag.astype(f32),
        *(jnp.ones((1, rows), f32) for _ in range(3)),
    )
    place_of = feature - (slot & 1) * HALF
    for n, value in enumerate(values):
        table = jnp.where(place_of == n, value, table)
    table = table.T
    column = iota((rows, LANES), 1) & (HALF - 1)
    nothing = jnp.zeros((rows, LANES), bf16)

    def block(c):
        return ref_ref[:, c * LANES : (c + 1) * LANES] if c < blocks else nothing

    half = tall - 8
    row = iota((OCTET, half, rows), 1)
    place = iota((OCTET, half, rows), 0) * cap + row
    pickers = []
    for o in range(owners // OCTET):
        for side in range(2):
            parts = []
            for c in range(2 * side, 2 * side + 2):
                first = c * cap - 8 * side
                mine = (row >= first) & (row < first + cap)
                hit = mine & (place + (o * OCTET * cap - first) == slot.reshape(1, 1, rows))
                parts.append(hit.astype(f32).reshape(OCTET * half, rows).astype(bf16))
            pickers.append(jnp.concatenate(parts, axis=1))
    pickers = [jnp.concatenate(pickers[side::2], axis=0) for side in range(2)]
    last_row = iota((owners, half, LANES), 1)
    tops, sums = [], []
    for n, g in enumerate(range(0, full, 2)):
        for copy in loads[:1] if n == 0 else loads[1:] if n == 1 else ():
            copy.wait()
        here = [block(c) for c in range(g * GROUP, min((g + 2) * GROUP, blocks))]
        tops.append(jnp.max(functools.reduce(jnp.maximum, here).astype(f32), axis=1, keepdims=True))
        level = jnp.broadcast_to(tops[-1], (rows, LANES))
        sums.append(jnp.sum(sum(jnp.exp(x.astype(f32) - level) for x in here), axis=1, keepdims=True))
        right = [
            jnp.concatenate(
                [
                    jnp.concatenate([block((g + h) * GROUP + 2 * side + c) for h in range(2)], axis=1)
                    for c in range(2)
                ],
                axis=0,
            )
            for side in range(2)
        ]
        out = [
            jnp.dot(pickers[side], right[side], preferred_element_type=f32).reshape(owners, half, 2 * LANES)
            for side in range(2)
        ]
        both = jnp.concatenate([out[0][:, 0:8], out[0][:, 8:] + out[1][:, : half - 8], out[1][:, half - 8 :]], axis=1)
        for h in range(min(2, full - g)):
            send_ref[:, (g + h) * tall : (g + h + 1) * tall, :] = both[:, :, h * LANES : (h + 1) * LANES].astype(bf16)
        if g + 2 > full:
            tail = out[0][:, :, LANES:]
    top = functools.reduce(jnp.maximum, tops)
    rest = top + jnp.log(sum(x * jnp.exp(t - top) for x, t in zip(sums, tops)))
    for n in range(len(values) - 3, len(values)):
        part = rest.astype(bf16).astype(f32)
        table = jnp.where(column == n, table * part, table)
        rest = rest - part
    table = table.astype(bf16)
    wide_row = iota((owners, half, rows), 1)
    pair = iota((owners, half, rows), 0) * (cap // 2) + wide_row - 2 * cap
    hit = (wide_row >= 2 * cap) & (wide_row < half - 1) & (pair == (slot >> 1).reshape(1, 1, rows))
    picker = hit.astype(f32).reshape(owners * half, rows).astype(bf16)
    extra = jnp.dot(picker, table, preferred_element_type=f32).reshape(owners, half, LANES)
    tail = jnp.where(last_row == half - 1, count.astype(f32), tail + extra)
    send_ref[:, full * tall :, :] = tail.astype(bf16)


def partial_kernel(cap, got_ref, pol_ref, exp_ref, gap_ref, part_ref, meta_ref, column_ref):
    slots, columns = pol_ref.shape
    blocks = columns // LANES
    owners = got_ref.shape[0]
    tall = GROUP * cap
    wide = OCTET * cap
    full = blocks // GROUP
    half = tall - 8
    base = lax.axis_index("tp") * columns

    size = OCTET * tall
    a = iota((GROUP, wide, size), 0)
    b = iota((GROUP, wide, size), 1)
    target = b + cap * a
    for d in range(1, OCTET):
        target = target + jnp.where(b >= d * cap, tall - cap, 0)
    order = (target == iota((GROUP, wide, size), 2)).astype(f32).reshape(size, size).astype(bf16)
    small = OCTET * half
    a = iota((3, wide, small), 0)
    b = iota((3, wide, small), 1)
    slot_row = b
    source = jnp.zeros_like(b)
    for d in range(1, OCTET):
        slot_row = slot_row - jnp.where(b >= d * cap, cap, 0)
        source = source + jnp.where(b >= d * cap, half, 0)
    source = source + jnp.where(a == 2, 2 * cap + (slot_row >> 1), a * cap + slot_row)
    tail_order = (source == iota((3, wide, small), 2)).astype(f32).reshape(3 * wide, small).astype(bf16)
    lane = iota((wide, LANES), 1)
    odd = (iota((wide, LANES), 0) & 1) == 1
    counts = jnp.zeros((1, LANES), f32)

    for o in range(owners // OCTET):
        at = slice(o * wide, (o + 1) * wide)
        highest = pol_ref[at, 0:LANES]
        for c in range(1, blocks):
            highest = jnp.maximum(highest, pol_ref[at, c * LANES : (c + 1) * LANES])
        peak = jnp.max(highest.astype(f32), axis=1, keepdims=True)
        peaks = jnp.broadcast_to(peak, (wide, LANES))

        def arrived(first, rows, ways, matrix):
            parts = [
                got_ref[o * OCTET : (o + 1) * OCTET, first + h * rows : first + (h + 1) * rows, :]
                .astype(f32)
                .reshape(OCTET * rows, LANES)
                .astype(bf16)
                for h in range(ways)
            ]
            right = jnp.concatenate(parts, axis=1) if ways > 1 else parts[0]
            return jnp.dot(matrix, right, preferred_element_type=f32)

        product = arrived(full * tall, half, 1, tail_order)
        todo = [{full * GROUP + c: product[c * wide : (c + 1) * wide] for c in range(2)}]
        info = product[2 * wide :]
        info = jnp.where(odd, pltpu.roll(info, HALF, 1), info)
        last = got_ref[o * OCTET : (o + 1) * OCTET, full * tall + 8 :, :].astype(f32)
        counts = counts + jnp.sum(last[:, half - 9, :], axis=0, keepdims=True)
        column = (info[:, 0:1] + 256.0 * info[:, 1:2] + 65536.0 * info[:, 2:3]).astype(i32) - base
        token = jnp.broadcast_to(column, (wide, LANES)) - lane
        total, cross, picked = (jnp.zeros((wide, LANES), f32) for _ in range(3))
        for g in range(full - 1, -1, -2):
            ways = 2 if g else 1
            product = arrived((g - ways + 1) * tall, tall, ways, order)
            todo.append(
                {
                    (g - ways + 1 + h) * GROUP + c: product[c * wide : (c + 1) * wide, h * LANES : (h + 1) * LANES]
                    for h in range(ways)
                    for c in range(GROUP)
                }
            )
        for pieces in todo:
            for c in sorted(pieces):
                q = pieces[c]
                span = slice(c * LANES, (c + 1) * LANES)
                z = pol_ref[at, span].astype(f32)
                exps = jnp.exp(z - peaks)
                gaps = exps * (z - q)
                exp_ref[at, span] = exps
                gap_ref[at, span] = gaps
                total = total + exps
                cross = cross + gaps
                picked = jnp.where(token == c * LANES, z, picked)
        sums = (
            peak,
            jnp.sum(total, axis=1, keepdims=True),
            jnp.sum(cross, axis=1, keepdims=True),
            jnp.sum(picked, axis=1, keepdims=True),
            info[:, 5:6] + info[:, 6:7] + info[:, 7:8],
            info[:, 3:4],
            info[:, 4:5],
            column.astype(f32),
        )
        out = jnp.zeros((wide, LANES), f32)
        for n, value in enumerate(sums):
            out = jnp.where(lane == n, value, out)
        column_ref[at, :] = out
    column_ref[slots:, :] = jnp.ones((column_ref.shape[0] - slots, LANES), f32)
    turned = column_ref[...].T
    peak, total, cross, picked, log_q = (turned[n : n + 1, :] for n in range(5))
    pairs = ((peak + jnp.log(total), cross / total), (picked, log_q))
    for n, pair in enumerate(pairs):
        line = jnp.concatenate([value[:, :slots] for value in pair], axis=1)
        part_ref[:, n : n + 1, :] = jnp.broadcast_to(line[None], (part_ref.shape[0],) + line.shape)
    for n in range(3):
        meta_ref[n : n + 1, :] = turned[5 + n : 6 + n, :]
    meta_ref[3:4, :] = jnp.concatenate([counts] * (meta_ref.shape[1] // LANES), axis=1)
    meta_ref[4:5, :] = peak


def grad_kernel(
    row_total, all_ref, meta_ref, rewards_ref, group_ref, exp_ref, gap_ref, grad_hbm, loss_ref, turn_ref, column_ref, grad_ref, store
):
    slots, columns = exp_ref.shape
    blocks = columns // LANES
    seqs = rewards_ref.shape[0]

    rewards = rewards_ref[...].reshape(1, seqs)
    groups = group_ref[...].reshape(1, seqs)
    diagonal = iota((seqs, seqs), 0) == iota((seqs, seqs), 1)
    group_down = jnp.sum(jnp.where(diagonal, groups, 0), axis=1, keepdims=True)
    reward_down = jnp.sum(jnp.where(diagonal, rewards, 0.0), axis=1, keepdims=True)
    same = (group_down == groups).astype(f32)
    mean = jnp.sum(same * rewards, axis=1, keepdims=True) / jnp.sum(same, axis=1, keepdims=True)
    advantage = reward_down - mean

    old, tag, token, valid_total, mine = (meta_ref[n : n + 1, :slots] for n in range(5))
    valid = tag > 0.5
    adv = jnp.sum(
        jnp.where(iota((seqs, slots), 0) + 1 == tag.astype(i32), advantage, 0.0), axis=0, keepdims=True
    )

    logs, gaps, tokens, logs_q = (all_ref[:, n, m * slots : (m + 1) * slots] for n in range(2) for m in range(2))
    peak = jnp.max(logs, axis=0, keepdims=True)
    weight = jnp.exp(logs - peak)
    total = jnp.sum(weight, axis=0, keepdims=True)
    gap = jnp.sum(gaps * weight, axis=0, keepdims=True) / total
    log_p = peak + jnp.log(total)
    peak_q = jnp.max(logs_q, axis=0, keepdims=True)
    log_q = peak_q + jnp.log(jnp.sum(jnp.exp(logs_q - peak_q), axis=0, keepdims=True))
    kl_term = gap - log_p + log_q
    raw = jnp.sum(tokens, axis=0, keepdims=True) - log_p - old
    ratio = jnp.exp(jnp.clip(raw, -ratio_clamp, ratio_clamp))
    plain = -adv * ratio
    clipped = -adv * jnp.clip(ratio, low_bound, high_bound)
    upper = jnp.maximum(plain, clipped)
    dual = -dual_bound * adv
    negative = adv < 0.0
    loss = jnp.where(negative, jnp.minimum(upper, dual), upper)
    loss_ref[...] = jnp.where(valid, loss + kl_weight * kl_term, 0.0).reshape(slots)
    inside = (ratio > low_bound) & (ratio < high_bound)
    coef = jnp.where((plain >= clipped) | inside, plain, 0.0)
    coef = jnp.where(negative & (upper > dual), 0.0, coef)
    coef = jnp.where(jnp.abs(raw) < ratio_clamp, coef, 0.0)
    scale = jnp.where(valid, row_total / valid_total, 0.0)
    turn_ref[...] = jnp.zeros(turn_ref.shape, f32)
    share = scale * jnp.exp(mine - peak) / total
    slope = share * kl_weight
    for n, value in enumerate((slope, slope * gap + share * coef, scale * coef, token)):
        turn_ref[n : n + 1, :slots] = value
    column_ref[...] = turn_ref[...].T
    step = slots // store.shape[0]
    lane = iota((step, LANES), 1)
    stores = []
    for i in range(slots // step):
        at = slice(i * step, (i + 1) * step)
        slope, level, spike, col = (
            jnp.broadcast_to(column_ref[at, n : n + 1], (step, LANES)) for n in range(4)
        )
        where = col.astype(i32) - lane
        for c in range(blocks):
            span = slice(c * LANES, (c + 1) * LANES)
            out = slope * gap_ref[at, span] - level * exp_ref[at, span]
            out = out + jnp.where(where == c * LANES, spike, 0.0)
            grad_ref[at, span] = out.astype(bf16)
        stores.append(pltpu.make_async_copy(grad_ref.at[at], grad_hbm.at[at], store.at[i]))
        stores[-1].start()
    for copy in stores:
        copy.wait()


def call(kernel, out_shape, ins, outs, scratch=(), cost=None, limit=VMEM_LIMIT):
    spec = {"h": pl.BlockSpec(memory_space=pltpu.HBM), "v": pl.BlockSpec(memory_space=pltpu.VMEM)}
    return pl.pallas_call(
        kernel,
        out_shape=out_shape,
        in_specs=[spec[n] for n in ins],
        out_specs=[spec[n] for n in outs],
        scratch_shapes=list(scratch),
        compiler_params=pltpu.CompilerParams(vmem_limit_bytes=limit),
        cost_estimate=cost,
    )


def shards(ref_logits, token_ids, old_logp, owner_of_row, lengths, rewards, group_ids, pol_logits):
    owners = lax.axis_size("role") * lax.axis_size("dp")
    return steps(owners, ref_logits, token_ids, old_logp, owner_of_row, lengths, rewards, group_ids, pol_logits)


def steps(owners, ref_logits, token_ids, old_logp, owner_of_row, lengths, rewards, group_ids, pol_logits):
    peers = lax.axis_size("tp")
    rows, columns = ref_logits.shape
    slots = pol_logits.shape[0]
    cap = slots // owners
    blocks = columns // LANES
    full = blocks // GROUP
    deep = blocks * cap + 4
    padded = -(-slots // LANES) * LANES
    shape = jax.ShapeDtypeStruct
    vmem = pltpu.VMEM
    sems = lambda n: pltpu.SemaphoreType.DMA((n,))
    everyone = ("role", "dp")

    [send] = call(
        functools.partial(send_kernel, cap),
        [shape((owners, deep, LANES), bf16)],
        "hhhhh",
        "v",
        (
            vmem((rows,), i32),
            vmem((rows,), bf16),
            vmem((rows,), i32),
            pltpu.SMEM(lengths.shape, i32),
            vmem((rows, columns), bf16),
            sems(4),
            sems(full // 2 + 1),
        ),
        limit=VMEM_LIMIT,
    )(*(pltpu.with_memory_space_constraint(x, pltpu.HBM) for x in (token_ids, old_logp, owner_of_row, lengths, ref_logits)))
    got = lax.all_to_all(send, everyone, split_axis=0, concat_axis=0, tiled=True)
    exps, gaps, parts, meta = call(
        functools.partial(partial_kernel, cap),
        [
            shape((slots, columns), f32),
            shape((slots, columns), f32),
            shape((peers, 2, 2 * slots), f32),
            shape((8, padded), f32),
        ],
        "vv",
        "vvvv",
        (vmem((padded, LANES), f32),),
    )(got, pol_logits)
    everything = lax.all_to_all(parts, "tp", split_axis=0, concat_axis=0, tiled=True)
    pieces = slots // STORE_ROWS
    return call(
        functools.partial(grad_kernel, float(rows * owners)),
        [shape((slots, columns), bf16), shape((slots,), f32)],
        "vvvvvv",
        "hv",
        (vmem((LANES, padded), f32), vmem((padded, LANES), f32), vmem((slots, columns), bf16), sems(pieces)),
    )(everything, meta, rewards, group_ids, exps, gaps)


def solution(mesh):
    return jax.shard_map(
        shards,
        mesh=mesh,
        in_specs=(
            P(("role", "dp"), "tp"),
            P(("role", "dp")),
            P(("role", "dp")),
            P(("role", "dp")),
            P(("role", "dp")),
            P(),
            P(),
            P(("role", "dp"), "tp"),
        ),
        out_specs=(P(("role", "dp"), "tp"), P(("role", "dp"))),
        check_vma=False,
    )
```

```python
import functools

import jax
import jax.numpy as jnp
from jax import lax
from jax.experimental import pallas as pl
from jax.experimental.pallas import tpu as pltpu
from jax.sharding import PartitionSpec as P

kl_weight = 0.04
low_bound = 0.8
high_bound = 1.2
dual_bound = 3.0
ratio_clamp = 20.0

LANES = 128
GROUP = 4
HALF = 64
OCTET = 8
STORE_ROWS = 16
VMEM_LIMIT = 16 * 1024 * 1024

f32 = jnp.float32
bf16 = jnp.bfloat16
i32 = jnp.int32


def iota(shape, dim):
    return lax.broadcasted_iota(i32, shape, dim)


def send_kernel(
    cap, ids_hbm, old_hbm, owner_hbm, len_hbm, ref_hbm, send_ref, ids_ref, old_ref, owner_ref, len_ref, ref_ref, small, load
):
    rows = ref_ref.shape[0]
    blocks = ref_ref.shape[1] // LANES
    owners = send_ref.shape[0]
    tall = GROUP * cap
    full = blocks // GROUP
    seq_local = len_ref.shape[0]
    span = rows // seq_local
    me = lax.axis_index("role") * lax.axis_size("dp") + lax.axis_index("dp")

    smalls = [
        pltpu.make_async_copy(source, target, small.at[n])
        for n, (source, target) in enumerate(
            ((owner_hbm, owner_ref), (ids_hbm, ids_ref), (old_hbm, old_ref), (len_hbm, len_ref))
        )
    ]
    loads = []
    for n, g in enumerate(range(0, full, 2)):
        part = slice(g * GROUP * LANES, min((g + 2) * GROUP, blocks) * LANES)
        loads.append(pltpu.make_async_copy(ref_hbm.at[:, part], ref_ref.at[:, part], load.at[n]))
    for copy in smalls + loads:
        copy.start()

    before = (iota((rows, rows), 0) < iota((rows, rows), 1)).astype(bf16)
    lane = iota((1, rows), 1)
    feature = iota((LANES, rows), 0)
    smalls[0].wait()
    owner = owner_ref[...].reshape(1, rows)
    hot = (iota((owners, rows), 0) == owner).astype(f32)
    earlier = jnp.dot(hot.astype(bf16), before, preferred_element_type=f32)
    rank = jnp.sum(earlier * hot, axis=0, keepdims=True).astype(i32)
    slot = owner * cap + rank

    for copy in smalls[1:]:
        copy.wait()
    tag = jnp.zeros((1, rows), i32)
    count = jnp.int32(0)
    for s in range(seq_local):
        length = len_ref[s]
        inside = (lane >= s * span) & (lane < s * span + jnp.minimum(length, span))
        tag = jnp.where(inside, me * seq_local + s + 1, tag)
        count = count + jnp.clip(length, 0, span)
    ids = ids_ref[...].reshape(1, rows)
    table = jnp.zeros((LANES, rows), f32)
    values = (
        (ids & 255).astype(f32),
        ((ids >> 8) & 255).astype(f32),
        (ids >> 16).astype(f32),
        old_ref[...].reshape(1, rows).astype(f32),
        tag.astype(f32),
        *(jnp.ones((1, rows), f32) for _ in range(3)),
    )
    place_of = feature - (slot & 1) * HALF
    for n, value in enumerate(values):
        table = jnp.where(place_of == n, value, table)
    table = table.T
    column = iota((rows, LANES), 1) & (HALF - 1)
    nothing = jnp.zeros((rows, LANES), bf16)

    def block(c):
        return ref_ref[:, c * LANES : (c + 1) * LANES] if c < blocks else nothing

    half = tall - 8
    row = iota((OCTET, half, rows), 1)
    place = iota((OCTET, half, rows), 0) * cap + row
    pickers = []
    for o in range(owners // OCTET):
        for side in range(2):
            parts = []
            for c in range(2 * side, 2 * side + 2):
                first = c * cap - 8 * side
                mine = (row >= first) & (row < first + cap)
                hit = mine & (place + (o * OCTET * cap - first) == slot.reshape(1, 1, rows))
                parts.append(hit.astype(f32).reshape(OCTET * half, rows).astype(bf16))
            pickers.append(jnp.concatenate(parts, axis=1))
    pickers = [jnp.concatenate(pickers[side::2], axis=0) for side in range(2)]
    last_row = iota((owners, half, LANES), 1)
    tops, sums = [], []
    for n, g in enumerate(range(0, full, 2)):
        for copy in loads[:1] if n == 0 else loads[1:] if n == 1 else ():
            copy.wait()
        if n < 2:
            here = [block(c) for c in range(0, 2 * GROUP) if c < blocks] if n == 0 else [block(c) for c in range(2 * GROUP, blocks)]
            tops.append(jnp.max(functools.reduce(jnp.maximum, here).astype(f32), axis=1, keepdims=True))
            level = jnp.broadcast_to(tops[-1], (rows, LANES))
            sums.append(jnp.sum(sum(jnp.exp(x.astype(f32) - level) for x in here), axis=1, keepdims=True))
        right = [
            jnp.concatenate(
                [
                    jnp.concatenate([block((g + h) * GROUP + 2 * side + c) for h in range(2)], axis=1)
                    for c in range(2)
                ],
                axis=0,
            )
            for side in range(2)
        ]
        out = [
            jnp.dot(pickers[side], right[side], preferred_element_type=f32).reshape(owners, half, 2 * LANES)
            for side in range(2)
        ]
        both = jnp.concatenate([out[0][:, 0:8], out[0][:, 8:] + out[1][:, : half - 8], out[1][:, half - 8 :]], axis=1)
        for h in range(min(2, full - g)):
            send_ref[:, (g + h) * tall : (g + h + 1) * tall, :] = both[:, :, h * LANES : (h + 1) * LANES].astype(bf16)
        if g + 2 > full:
            tail = out[0][:, :, LANES:]
    top = functools.reduce(jnp.maximum, tops)
    rest = top + jnp.log(sum(x * jnp.exp(t - top) for x, t in zip(sums, tops)))
    for n in range(len(values) - 3, len(values)):
        part = rest.astype(bf16).astype(f32)
        table = jnp.where(column == n, table * part, table)
        rest = rest - part
    table = table.astype(bf16)
    wide_row = iota((owners, half, rows), 1)
    pair = iota((owners, half, rows), 0) * (cap // 2) + wide_row - 2 * cap
    hit = (wide_row >= 2 * cap) & (wide_row < half - 1) & (pair == (slot >> 1).reshape(1, 1, rows))
    picker = hit.astype(f32).reshape(owners * half, rows).astype(bf16)
    extra = jnp.dot(picker, table, preferred_element_type=f32).reshape(owners, half, LANES)
    tail = jnp.where(last_row == half - 1, count.astype(f32), tail + extra)
    send_ref[:, full * tall :, :] = tail.astype(bf16)


def partial_kernel(cap, got_ref, pol_ref, exp_ref, gap_ref, part_ref, meta_ref, column_ref):
    slots, columns = pol_ref.shape
    blocks = columns // LANES
    owners = got_ref.shape[0]
    tall = GROUP * cap
    wide = OCTET * cap
    full = blocks // GROUP
    half = tall - 8
    base = lax.axis_index("tp") * columns

    size = OCTET * tall
    a = iota((GROUP, wide, size), 0)
    b = iota((GROUP, wide, size), 1)
    target = b + cap * a
    for d in range(1, OCTET):
        target = target + jnp.where(b >= d * cap, tall - cap, 0)
    order = (target == iota((GROUP, wide, size), 2)).astype(f32).reshape(size, size).astype(bf16)
    small = OCTET * half
    a = iota((3, wide, small), 0)
    b = iota((3, wide, small), 1)
    slot_row = b
    source = jnp.zeros_like(b)
    for d in range(1, OCTET):
        slot_row = slot_row - jnp.where(b >= d * cap, cap, 0)
        source = source + jnp.where(b >= d * cap, half, 0)
    source = source + jnp.where(a == 2, 2 * cap + (slot_row >> 1), a * cap + slot_row)
    tail_order = (source == iota((3, wide, small), 2)).astype(f32).reshape(3 * wide, small).astype(bf16)
    lane = iota((wide, LANES), 1)
    odd = (iota((wide, LANES), 0) & 1) == 1
    counts = jnp.zeros((1, LANES), f32)

    for o in range(owners // OCTET):
        at = slice(o * wide, (o + 1) * wide)
        highest = pol_ref[at, 0:LANES]
        for c in range(1, blocks):
            highest = jnp.maximum(highest, pol_ref[at, c * LANES : (c + 1) * LANES])
        peak = jnp.max(highest.astype(f32), axis=1, keepdims=True)
        peaks = jnp.broadcast_to(peak, (wide, LANES))

        def arrived(first, rows, ways, matrix):
            parts = [
                got_ref[o * OCTET : (o + 1) * OCTET, first + h * rows : first + (h + 1) * rows, :]
                .astype(f32)
                .reshape(OCTET * rows, LANES)
                .astype(bf16)
                for h in range(ways)
            ]
            right = jnp.concatenate(parts, axis=1) if ways > 1 else parts[0]
            return jnp.dot(matrix, right, preferred_element_type=f32)

        product = arrived(full * tall, half, 1, tail_order)
        todo = [{full * GROUP + c: product[c * wide : (c + 1) * wide] for c in range(2)}]
        info = product[2 * wide :]
        info = jnp.where(odd, pltpu.roll(info, HALF, 1), info)
        last = got_ref[o * OCTET : (o + 1) * OCTET, full * tall + 8 :, :].astype(f32)
        counts = counts + jnp.sum(last[:, half - 9, :], axis=0, keepdims=True)
        column = (info[:, 0:1] + 256.0 * info[:, 1:2] + 65536.0 * info[:, 2:3]).astype(i32) - base
        token = jnp.broadcast_to(column, (wide, LANES)) - lane
        total, cross, picked = (jnp.zeros((wide, LANES), f32) for _ in range(3))
        for g in range(full - 1, -1, -2):
            ways = 2 if g else 1
            product = arrived((g - ways + 1) * tall, tall, ways, order)
            todo.append(
                {
                    (g - ways + 1 + h) * GROUP + c: product[c * wide : (c + 1) * wide, h * LANES : (h + 1) * LANES]
                    for h in range(ways)
                    for c in range(GROUP)
                }
            )
        for pieces in todo:
            for c in sorted(pieces):
                q = pieces[c]
                span = slice(c * LANES, (c + 1) * LANES)
                z = pol_ref[at, span].astype(f32)
                exps = jnp.exp(z - peaks)
                gaps = exps * (z - q)
                exp_ref[at, span] = exps
                gap_ref[at, span] = gaps
                total = total + exps
                cross = cross + gaps
                picked = jnp.where(token == c * LANES, z, picked)
        sums = (
            peak,
            jnp.sum(total, axis=1, keepdims=True),
            jnp.sum(cross, axis=1, keepdims=True),
            jnp.sum(picked, axis=1, keepdims=True),
            info[:, 5:6] + info[:, 6:7] + info[:, 7:8],
            info[:, 3:4],
            info[:, 4:5],
            column.astype(f32),
        )
        out = jnp.zeros((wide, LANES), f32)
        for n, value in enumerate(sums):
            out = jnp.where(lane == n, value, out)
        column_ref[at, :] = out
    column_ref[slots:, :] = jnp.ones((column_ref.shape[0] - slots, LANES), f32)
    turned = column_ref[...].T
    peak, total, cross, picked, log_q = (turned[n : n + 1, :] for n in range(5))
    pairs = ((peak + jnp.log(total), cross / total), (picked, log_q))
    for n, pair in enumerate(pairs):
        line = jnp.concatenate([value[:, :slots] for value in pair], axis=1)
        part_ref[:, n : n + 1, :] = jnp.broadcast_to(line[None], (part_ref.shape[0],) + line.shape)
    for n in range(3):
        meta_ref[n : n + 1, :] = turned[5 + n : 6 + n, :]
    meta_ref[3:4, :] = jnp.concatenate([counts] * (meta_ref.shape[1] // LANES), axis=1)
    meta_ref[4:5, :] = peak


def grad_kernel(
    row_total, all_ref, meta_ref, rewards_ref, group_ref, exp_ref, gap_ref, grad_hbm, loss_ref, turn_ref, column_ref, grad_ref, store
):
    slots, columns = exp_ref.shape
    blocks = columns // LANES
    seqs = rewards_ref.shape[0]

    rewards = rewards_ref[...].reshape(1, seqs)
    groups = group_ref[...].reshape(1, seqs)
    diagonal = iota((seqs, seqs), 0) == iota((seqs, seqs), 1)
    group_down = jnp.sum(jnp.where(diagonal, groups, 0), axis=1, keepdims=True)
    reward_down = jnp.sum(jnp.where(diagonal, rewards, 0.0), axis=1, keepdims=True)
    same = (group_down == groups).astype(f32)
    mean = jnp.sum(same * rewards, axis=1, keepdims=True) / jnp.sum(same, axis=1, keepdims=True)
    advantage = reward_down - mean

    old, tag, token, valid_total, mine = (meta_ref[n : n + 1, :slots] for n in range(5))
    valid = tag > 0.5
    adv = jnp.sum(
        jnp.where(iota((seqs, slots), 0) + 1 == tag.astype(i32), advantage, 0.0), axis=0, keepdims=True
    )

    logs, gaps, tokens, logs_q = (all_ref[:, n, m * slots : (m + 1) * slots] for n in range(2) for m in range(2))
    peak = jnp.max(logs, axis=0, keepdims=True)
    weight = jnp.exp(logs - peak)
    total = jnp.sum(weight, axis=0, keepdims=True)
    gap = jnp.sum(gaps * weight, axis=0, keepdims=True) / total
    log_p = peak + jnp.log(total)
    peak_q = jnp.max(logs_q, axis=0, keepdims=True)
    log_q = peak_q + jnp.log(jnp.sum(jnp.exp(logs_q - peak_q), axis=0, keepdims=True))
    kl_term = gap - log_p + log_q
    raw = jnp.sum(tokens, axis=0, keepdims=True) - log_p - old
    ratio = jnp.exp(jnp.clip(raw, -ratio_clamp, ratio_clamp))
    plain = -adv * ratio
    clipped = -adv * jnp.clip(ratio, low_bound, high_bound)
    upper = jnp.maximum(plain, clipped)
    dual = -dual_bound * adv
    negative = adv < 0.0
    loss = jnp.where(negative, jnp.minimum(upper, dual), upper)
    loss_ref[...] = jnp.where(valid, loss + kl_weight * kl_term, 0.0).reshape(slots)
    inside = (ratio > low_bound) & (ratio < high_bound)
    coef = jnp.where((plain >= clipped) | inside, plain, 0.0)
    coef = jnp.where(negative & (upper > dual), 0.0, coef)
    coef = jnp.where(jnp.abs(raw) < ratio_clamp, coef, 0.0)
    scale = jnp.where(valid, row_total / valid_total, 0.0)
    turn_ref[...] = jnp.zeros(turn_ref.shape, f32)
    share = scale * jnp.exp(mine - peak) / total
    slope = share * kl_weight
    for n, value in enumerate((slope, slope * gap + share * coef, scale * coef, token)):
        turn_ref[n : n + 1, :slots] = value
    column_ref[...] = turn_ref[...].T
    step = slots // store.shape[0]
    lane = iota((step, LANES), 1)
    stores = []
    for i in range(slots // step):
        at = slice(i * step, (i + 1) * step)
        slope, level, spike, col = (
            jnp.broadcast_to(column_ref[at, n : n + 1], (step, LANES)) for n in range(4)
        )
        where = col.astype(i32) - lane
        for c in range(blocks):
            span = slice(c * LANES, (c + 1) * LANES)
            out = slope * gap_ref[at, span] - level * exp_ref[at, span]
            out = out + jnp.where(where == c * LANES, spike, 0.0)
            grad_ref[at, span] = out.astype(bf16)
        stores.append(pltpu.make_async_copy(grad_ref.at[at], grad_hbm.at[at], store.at[i]))
        stores[-1].start()
    for copy in stores:
        copy.wait()


def call(kernel, out_shape, ins, outs, scratch=(), cost=None, limit=VMEM_LIMIT):
    spec = {"h": pl.BlockSpec(memory_space=pltpu.HBM), "v": pl.BlockSpec(memory_space=pltpu.VMEM)}
    return pl.pallas_call(
        kernel,
        out_shape=out_shape,
        in_specs=[spec[n] for n in ins],
        out_specs=[spec[n] for n in outs],
        scratch_shapes=list(scratch),
        compiler_params=pltpu.CompilerParams(vmem_limit_bytes=limit),
        cost_estimate=cost,
    )


def shards(ref_logits, token_ids, old_logp, owner_of_row, lengths, rewards, group_ids, pol_logits):
    owners = lax.axis_size("role") * lax.axis_size("dp")
    return steps(owners, ref_logits, token_ids, old_logp, owner_of_row, lengths, rewards, group_ids, pol_logits)


def steps(owners, ref_logits, token_ids, old_logp, owner_of_row, lengths, rewards, group_ids, pol_logits):
    peers = lax.axis_size("tp")
    rows, columns = ref_logits.shape
    slots = pol_logits.shape[0]
    cap = slots // owners
    blocks = columns // LANES
    full = blocks // GROUP
    deep = blocks * cap + 4
    padded = -(-slots // LANES) * LANES
    shape = jax.ShapeDtypeStruct
    vmem = pltpu.VMEM
    sems = lambda n: pltpu.SemaphoreType.DMA((n,))
    everyone = ("role", "dp")

    [send] = call(
        functools.partial(send_kernel, cap),
        [shape((owners, deep, LANES), bf16)],
        "hhhhh",
        "v",
        (
            vmem((rows,), i32),
            vmem((rows,), bf16),
            vmem((rows,), i32),
            pltpu.SMEM(lengths.shape, i32),
            vmem((rows, columns), bf16),
            sems(4),
            sems(full // 2 + 1),
        ),
        limit=VMEM_LIMIT,
    )(*(pltpu.with_memory_space_constraint(x, pltpu.HBM) for x in (token_ids, old_logp, owner_of_row, lengths, ref_logits)))
    got = lax.all_to_all(send, everyone, split_axis=0, concat_axis=0, tiled=True)
    exps, gaps, parts, meta = call(
        functools.partial(partial_kernel, cap),
        [
            shape((slots, columns), f32),
            shape((slots, columns), f32),
            shape((peers, 2, 2 * slots), f32),
            shape((8, padded), f32),
        ],
        "vv",
        "vvvv",
        (vmem((padded, LANES), f32),),
    )(got, pol_logits)
    everything = lax.all_to_all(parts, "tp", split_axis=0, concat_axis=0, tiled=True)
    pieces = slots // STORE_ROWS
    return call(
        functools.partial(grad_kernel, float(rows * owners)),
        [shape((slots, columns), bf16), shape((slots,), f32)],
        "vvvvvv",
        "hv",
        (vmem((LANES, padded), f32), vmem((padded, LANES), f32), vmem((slots, columns), bf16), sems(pieces)),
    )(everything, meta, rewards, group_ids, exps, gaps)


def solution(mesh):
    return jax.shard_map(
        shards,
        mesh=mesh,
        in_specs=(
            P(("role", "dp"), "tp"),
            P(("role", "dp")),
            P(("role", "dp")),
            P(("role", "dp")),
            P(("role", "dp")),
            P(),
            P(),
            P(("role", "dp"), "tp"),
        ),
        out_specs=(P(("role", "dp"), "tp"), P(("role", "dp"))),
        check_vma=False,
    )
```

```python
import functools

import jax
import jax.numpy as jnp
from jax import lax
from jax.experimental import pallas as pl
from jax.experimental.pallas import tpu as pltpu
from jax.sharding import PartitionSpec as P

kl_weight = 0.04
low_bound = 0.8
high_bound = 1.2
dual_bound = 3.0
ratio_clamp = 20.0

LANES = 128
GROUP = 4
HALF = 64
OCTET = 8
STORE_ROWS = 16
VMEM_LIMIT = 16 * 1024 * 1024

f32 = jnp.float32
bf16 = jnp.bfloat16
i32 = jnp.int32


def iota(shape, dim):
    return lax.broadcasted_iota(i32, shape, dim)


def send_kernel(
    cap, ids_hbm, old_hbm, owner_hbm, len_hbm, ref_hbm, send_ref, ids_ref, old_ref, owner_ref, len_ref, ref_ref, small, load
):
    rows = ref_ref.shape[0]
    blocks = ref_ref.shape[1] // LANES
    owners = send_ref.shape[0]
    tall = GROUP * cap
    full = blocks // GROUP
    seq_local = len_ref.shape[0]
    span = rows // seq_local
    me = lax.axis_index("role") * lax.axis_size("dp") + lax.axis_index("dp")

    smalls = [
        pltpu.make_async_copy(source, target, small.at[n])
        for n, (source, target) in enumerate(
            ((owner_hbm, owner_ref), (ids_hbm, ids_ref), (old_hbm, old_ref), (len_hbm, len_ref))
        )
    ]
    loads = []
    first = min(2 * GROUP, blocks) * LANES
    for n, part in enumerate((slice(0, first), slice(first, blocks * LANES))[: 1 + (blocks > 2 * GROUP)]):
        loads.append(pltpu.make_async_copy(ref_hbm.at[:, part], ref_ref.at[:, part], load.at[n]))
    for copy in smalls + loads:
        copy.start()

    before = (iota((rows, rows), 0) < iota((rows, rows), 1)).astype(bf16)
    lane = iota((1, rows), 1)
    feature = iota((LANES, rows), 0)
    smalls[0].wait()
    owner = owner_ref[...].reshape(1, rows)
    hot = (iota((owners, rows), 0) == owner).astype(f32)
    earlier = jnp.dot(hot.astype(bf16), before, preferred_element_type=f32)
    rank = jnp.sum(earlier * hot, axis=0, keepdims=True).astype(i32)
    slot = owner * cap + rank

    for copy in smalls[1:]:
        copy.wait()
    tag = jnp.zeros((1, rows), i32)
    count = jnp.int32(0)
    for s in range(seq_local):
        length = len_ref[s]
        inside = (lane >= s * span) & (lane < s * span + jnp.minimum(length, span))
        tag = jnp.where(inside, me * seq_local + s + 1, tag)
        count = count + jnp.clip(length, 0, span)
    ids = ids_ref[...].reshape(1, rows)
    table = jnp.zeros((LANES, rows), f32)
    values = (
        (ids & 255).astype(f32),
        ((ids >> 8) & 255).astype(f32),
        (ids >> 16).astype(f32),
        old_ref[...].reshape(1, rows).astype(f32),
        tag.astype(f32),
        *(jnp.ones((1, rows), f32) for _ in range(3)),
    )
    place_of = feature - (slot & 1) * HALF
    for n, value in enumerate(values):
        table = jnp.where(place_of == n, value, table)
    table = table.T
    column = iota((rows, LANES), 1) & (HALF - 1)
    nothing = jnp.zeros((rows, LANES), bf16)

    def block(c):
        return ref_ref[:, c * LANES : (c + 1) * LANES] if c < blocks else nothing

    half = tall - 8
    row = iota((OCTET, half, rows), 1)
    place = iota((OCTET, half, rows), 0) * cap + row
    pickers = []
    for o in range(owners // OCTET):
        for side in range(2):
            parts = []
            for c in range(2 * side, 2 * side + 2):
                first = c * cap - 8 * side
                mine = (row >= first) & (row < first + cap)
                hit = mine & (place + (o * OCTET * cap - first) == slot.reshape(1, 1, rows))
                parts.append(hit.astype(f32).reshape(OCTET * half, rows).astype(bf16))
            pickers.append(jnp.concatenate(parts, axis=1))
    pickers = [jnp.concatenate(pickers[side::2], axis=0) for side in range(2)]
    last_row = iota((owners, half, LANES), 1)
    tops, sums = [], []
    for n, g in enumerate(range(0, full, 2)):
        for copy in loads[:1] if n == 0 else loads[1:] if n == 1 else ():
            copy.wait()
        if n < 2:
            here = [block(c) for c in range(0, 2 * GROUP) if c < blocks] if n == 0 else [block(c) for c in range(2 * GROUP, blocks)]
            tops.append(jnp.max(functools.reduce(jnp.maximum, here).astype(f32), axis=1, keepdims=True))
            level = jnp.broadcast_to(tops[-1], (rows, LANES))
            sums.append(jnp.sum(sum(jnp.exp(x.astype(f32) - level) for x in here), axis=1, keepdims=True))
        right = [
            jnp.concatenate(
                [
                    jnp.concatenate([block((g + h) * GROUP + 2 * side + c) for h in range(2)], axis=1)
                    for c in range(2)
                ],
                axis=0,
            )
            for side in range(2)
        ]
        out = [
            jnp.dot(pickers[side], right[side], preferred_element_type=f32).reshape(owners, half, 2 * LANES)
            for side in range(2)
        ]
        both = jnp.concatenate([out[0][:, 0:8], out[0][:, 8:] + out[1][:, : half - 8], out[1][:, half - 8 :]], axis=1)
        for h in range(min(2, full - g)):
            send_ref[:, (g + h) * tall : (g + h + 1) * tall, :] = both[:, :, h * LANES : (h + 1) * LANES].astype(bf16)
        if g + 2 > full:
            tail = out[0][:, :, LANES:]
    top = functools.reduce(jnp.maximum, tops)
    rest = top + jnp.log(sum(x * jnp.exp(t - top) for x, t in zip(sums, tops)))
    for n in range(len(values) - 3, len(values)):
        part = rest.astype(bf16).astype(f32)
        table = jnp.where(column == n, table * part, table)
        rest = rest - part
    table = table.astype(bf16)
    wide_row = iota((owners, half, rows), 1)
    pair = iota((owners, half, rows), 0) * (cap // 2) + wide_row - 2 * cap
    hit = (wide_row >= 2 * cap) & (wide_row < half - 1) & (pair == (slot >> 1).reshape(1, 1, rows))
    picker = hit.astype(f32).reshape(owners * half, rows).astype(bf16)
    extra = jnp.dot(picker, table, preferred_element_type=f32).reshape(owners, half, LANES)
    tail = jnp.where(last_row == half - 1, count.astype(f32), tail + extra)
    send_ref[:, full * tall :, :] = tail.astype(bf16)


def partial_kernel(cap, got_ref, pol_ref, exp_ref, gap_ref, part_ref, meta_ref, column_ref):
    slots, columns = pol_ref.shape
    blocks = columns // LANES
    owners = got_ref.shape[0]
    tall = GROUP * cap
    wide = OCTET * cap
    full = blocks // GROUP
    half = tall - 8
    base = lax.axis_index("tp") * columns

    size = OCTET * tall
    a = iota((GROUP, wide, size), 0)
    b = iota((GROUP, wide, size), 1)
    target = b + cap * a
    for d in range(1, OCTET):
        target = target + jnp.where(b >= d * cap, tall - cap, 0)
    order = (target == iota((GROUP, wide, size), 2)).astype(f32).reshape(size, size).astype(bf16)
    small = OCTET * half
    a = iota((3, wide, small), 0)
    b = iota((3, wide, small), 1)
    slot_row = b
    source = jnp.zeros_like(b)
    for d in range(1, OCTET):
        slot_row = slot_row - jnp.where(b >= d * cap, cap, 0)
        source = source + jnp.where(b >= d * cap, half, 0)
    source = source + jnp.where(a == 2, 2 * cap + (slot_row >> 1), a * cap + slot_row)
    tail_order = (source == iota((3, wide, small), 2)).astype(f32).reshape(3 * wide, small).astype(bf16)
    lane = iota((wide, LANES), 1)
    odd = (iota((wide, LANES), 0) & 1) == 1
    counts = jnp.zeros((1, LANES), f32)

    for o in range(owners // OCTET):
        at = slice(o * wide, (o + 1) * wide)
        highest = pol_ref[at, 0:LANES]
        for c in range(1, blocks):
            highest = jnp.maximum(highest, pol_ref[at, c * LANES : (c + 1) * LANES])
        peak = jnp.max(highest.astype(f32), axis=1, keepdims=True)
        peaks = jnp.broadcast_to(peak, (wide, LANES))

        def arrived(first, rows, ways, matrix):
            parts = [
                got_ref[o * OCTET : (o + 1) * OCTET, first + h * rows : first + (h + 1) * rows, :]
                .astype(f32)
                .reshape(OCTET * rows, LANES)
                .astype(bf16)
                for h in range(ways)
            ]
            right = jnp.concatenate(parts, axis=1) if ways > 1 else parts[0]
            return jnp.dot(matrix, right, preferred_element_type=f32)

        product = arrived(full * tall, half, 1, tail_order)
        todo = [{full * GROUP + c: product[c * wide : (c + 1) * wide] for c in range(2)}]
        info = product[2 * wide :]
        info = jnp.where(odd, pltpu.roll(info, HALF, 1), info)
        last = got_ref[o * OCTET : (o + 1) * OCTET, full * tall + 8 :, :].astype(f32)
        counts = counts + jnp.sum(last[:, half - 9, :], axis=0, keepdims=True)
        column = (info[:, 0:1] + 256.0 * info[:, 1:2] + 65536.0 * info[:, 2:3]).astype(i32) - base
        token = jnp.broadcast_to(column, (wide, LANES)) - lane
        total, cross, picked = (jnp.zeros((wide, LANES), f32) for _ in range(3))
        for g in range(full - 1, -1, -2):
            ways = 2 if g else 1
            product = arrived((g - ways + 1) * tall, tall, ways, order)
            todo.append(
                {
                    (g - ways + 1 + h) * GROUP + c: product[c * wide : (c + 1) * wide, h * LANES : (h + 1) * LANES]
                    for h in range(ways)
                    for c in range(GROUP)
                }
            )
        for pieces in todo:
            for c in sorted(pieces):
                q = pieces[c]
                span = slice(c * LANES, (c + 1) * LANES)
                z = pol_ref[at, span].astype(f32)
                exps = jnp.exp(z - peaks)
                gaps = exps * (z - q)
                exp_ref[at, span] = exps
                gap_ref[at, span] = gaps
                total = total + exps
                cross = cross + gaps
                picked = jnp.where(token == c * LANES, z, picked)
        sums = (
            peak,
            jnp.sum(total, axis=1, keepdims=True),
            jnp.sum(cross, axis=1, keepdims=True),
            jnp.sum(picked, axis=1, keepdims=True),
            info[:, 5:6] + info[:, 6:7] + info[:, 7:8],
            info[:, 3:4],
            info[:, 4:5],
            column.astype(f32),
        )
        out = jnp.zeros((wide, LANES), f32)
        for n, value in enumerate(sums):
            out = jnp.where(lane == n, value, out)
        column_ref[at, :] = out
    column_ref[slots:, :] = jnp.ones((column_ref.shape[0] - slots, LANES), f32)
    turned = column_ref[...].T
    peak, total, cross, picked, log_q = (turned[n : n + 1, :] for n in range(5))
    pairs = ((peak + jnp.log(total), cross / total), (picked, log_q))
    for n, pair in enumerate(pairs):
        line = jnp.concatenate([value[:, :slots] for value in pair], axis=1)
        part_ref[:, n : n + 1, :] = jnp.broadcast_to(line[None], (part_ref.shape[0],) + line.shape)
    for n in range(3):
        meta_ref[n : n + 1, :] = turned[5 + n : 6 + n, :]
    meta_ref[3:4, :] = jnp.concatenate([counts] * (meta_ref.shape[1] // LANES), axis=1)
    meta_ref[4:5, :] = peak


def grad_kernel(
    row_total, all_ref, meta_ref, rewards_ref, group_ref, exp_ref, gap_ref, grad_hbm, loss_ref, turn_ref, column_ref, grad_ref, store
):
    slots, columns = exp_ref.shape
    blocks = columns // LANES
    seqs = rewards_ref.shape[0]

    rewards = rewards_ref[...].reshape(1, seqs)
    groups = group_ref[...].reshape(1, seqs)
    diagonal = iota((seqs, seqs), 0) == iota((seqs, seqs), 1)
    group_down = jnp.sum(jnp.where(diagonal, groups, 0), axis=1, keepdims=True)
    reward_down = jnp.sum(jnp.where(diagonal, rewards, 0.0), axis=1, keepdims=True)
    same = (group_down == groups).astype(f32)
    mean = jnp.sum(same * rewards, axis=1, keepdims=True) / jnp.sum(same, axis=1, keepdims=True)
    advantage = reward_down - mean

    old, tag, token, valid_total, mine = (meta_ref[n : n + 1, :slots] for n in range(5))
    valid = tag > 0.5
    adv = jnp.sum(
        jnp.where(iota((seqs, slots), 0) + 1 == tag.astype(i32), advantage, 0.0), axis=0, keepdims=True
    )

    logs, gaps, tokens, logs_q = (all_ref[:, n, m * slots : (m + 1) * slots] for n in range(2) for m in range(2))
    peak = jnp.max(logs, axis=0, keepdims=True)
    weight = jnp.exp(logs - peak)
    total = jnp.sum(weight, axis=0, keepdims=True)
    gap = jnp.sum(gaps * weight, axis=0, keepdims=True) / total
    log_p = peak + jnp.log(total)
    peak_q = jnp.max(logs_q, axis=0, keepdims=True)
    log_q = peak_q + jnp.log(jnp.sum(jnp.exp(logs_q - peak_q), axis=0, keepdims=True))
    kl_term = gap - log_p + log_q
    raw = jnp.sum(tokens, axis=0, keepdims=True) - log_p - old
    ratio = jnp.exp(jnp.clip(raw, -ratio_clamp, ratio_clamp))
    plain = -adv * ratio
    clipped = -adv * jnp.clip(ratio, low_bound, high_bound)
    upper = jnp.maximum(plain, clipped)
    dual = -dual_bound * adv
    negative = adv < 0.0
    loss = jnp.where(negative, jnp.minimum(upper, dual), upper)
    loss_ref[...] = jnp.where(valid, loss + kl_weight * kl_term, 0.0).reshape(slots)
    inside = (ratio > low_bound) & (ratio < high_bound)
    coef = jnp.where((plain >= clipped) | inside, plain, 0.0)
    coef = jnp.where(negative & (upper > dual), 0.0, coef)
    coef = jnp.where(jnp.abs(raw) < ratio_clamp, coef, 0.0)
    scale = jnp.where(valid, row_total / valid_total, 0.0)
    turn_ref[...] = jnp.zeros(turn_ref.shape, f32)
    share = scale * jnp.exp(mine - peak) / total
    slope = share * kl_weight
    for n, value in enumerate((slope, slope * gap + share * coef, scale * coef, token)):
        turn_ref[n : n + 1, :slots] = value
    column_ref[...] = turn_ref[...].T
    step = slots // store.shape[0]
    lane = iota((step, LANES), 1)
    stores = []
    for i in range(slots // step):
        at = slice(i * step, (i + 1) * step)
        slope, level, spike, col = (
            jnp.broadcast_to(column_ref[at, n : n + 1], (step, LANES)) for n in range(4)
        )
        where = col.astype(i32) - lane
        for c in range(blocks):
            span = slice(c * LANES, (c + 1) * LANES)
            out = slope * gap_ref[at, span] - level * exp_ref[at, span]
            out = out + jnp.where(where == c * LANES, spike, 0.0)
            grad_ref[at, span] = out.astype(bf16)
        stores.append(pltpu.make_async_copy(grad_ref.at[at], grad_hbm.at[at], store.at[i]))
        stores[-1].start()
    for copy in stores:
        copy.wait()


def call(kernel, out_shape, ins, outs, scratch=(), cost=None, limit=VMEM_LIMIT):
    spec = {"h": pl.BlockSpec(memory_space=pltpu.HBM), "v": pl.BlockSpec(memory_space=pltpu.VMEM)}
    return pl.pallas_call(
        kernel,
        out_shape=out_shape,
        in_specs=[spec[n] for n in ins],
        out_specs=[spec[n] for n in outs],
        scratch_shapes=list(scratch),
        compiler_params=pltpu.CompilerParams(vmem_limit_bytes=limit),
        cost_estimate=cost,
    )


def shards(ref_logits, token_ids, old_logp, owner_of_row, lengths, rewards, group_ids, pol_logits):
    owners = lax.axis_size("role") * lax.axis_size("dp")
    return steps(owners, ref_logits, token_ids, old_logp, owner_of_row, lengths, rewards, group_ids, pol_logits)


def steps(owners, ref_logits, token_ids, old_logp, owner_of_row, lengths, rewards, group_ids, pol_logits):
    peers = lax.axis_size("tp")
    rows, columns = ref_logits.shape
    slots = pol_logits.shape[0]
    cap = slots // owners
    blocks = columns // LANES
    full = blocks // GROUP
    deep = blocks * cap + 4
    padded = -(-slots // LANES) * LANES
    shape = jax.ShapeDtypeStruct
    vmem = pltpu.VMEM
    sems = lambda n: pltpu.SemaphoreType.DMA((n,))
    everyone = ("role", "dp")

    [send] = call(
        functools.partial(send_kernel, cap),
        [shape((owners, deep, LANES), bf16)],
        "hhhhh",
        "v",
        (
            vmem((rows,), i32),
            vmem((rows,), bf16),
            vmem((rows,), i32),
            pltpu.SMEM(lengths.shape, i32),
            vmem((rows, columns), bf16),
            sems(4),
            sems(2),
        ),
        limit=VMEM_LIMIT,
    )(*(pltpu.with_memory_space_constraint(x, pltpu.HBM) for x in (token_ids, old_logp, owner_of_row, lengths, ref_logits)))
    got = lax.all_to_all(send, everyone, split_axis=0, concat_axis=0, tiled=True)
    exps, gaps, parts, meta = call(
        functools.partial(partial_kernel, cap),
        [
            shape((slots, columns), f32),
            shape((slots, columns), f32),
            shape((peers, 2, 2 * slots), f32),
            shape((8, padded), f32),
        ],
        "vv",
        "vvvv",
        (vmem((padded, LANES), f32),),
    )(got, pol_logits)
    everything = lax.all_to_all(parts, "tp", split_axis=0, concat_axis=0, tiled=True)
    pieces = slots // STORE_ROWS
    return call(
        functools.partial(grad_kernel, float(rows * owners)),
        [shape((slots, columns), bf16), shape((slots,), f32)],
        "vvvvvv",
        "hv",
        (vmem((LANES, padded), f32), vmem((padded, LANES), f32), vmem((slots, columns), bf16), sems(pieces)),
    )(everything, meta, rewards, group_ids, exps, gaps)


def solution(mesh):
    return jax.shard_map(
        shards,
        mesh=mesh,
        in_specs=(
            P(("role", "dp"), "tp"),
            P(("role", "dp")),
            P(("role", "dp")),
            P(("role", "dp")),
            P(("role", "dp")),
            P(),
            P(),
            P(("role", "dp"), "tp"),
        ),
        out_specs=(P(("role", "dp"), "tp"), P(("role", "dp"))),
        check_vma=False,
    )
```
